512 devices in a mesh: seq: 32 (over x, z), tp: 16 (over y, core).
Axes of the slice: x: 4, y: 8, z: 8, core: 2. Of those that a mesh axis runs over, the one named last changes fastest.
Arguments:
- residual: bfloat16 [6144, 8192], P('seq', 'tp'), may hold values from -6 to 6
- attention: bfloat16 [1536, 8192], P('seq'), may hold values from -6 to 6
- quantized_codes: int32 [8192, 8192], P('seq', 'tp'), may hold values from 0 to 15
- absmax: float32 [8192, 128], P('seq', 'tp'), may hold values from 0.005 to 0.05
- adapter_down: bfloat16 [8192, 64], P('seq'), may hold values from -0.0625 to 0.0625
- adapter_up: bfloat16 [64, 8192], P(None, 'tp'), may hold values from -0.75 to 0.75
- routed_slot_gate: float32 [1536], P('seq'), may hold values from 0.2 to 1
- selected: int32 [1536], P('seq'), may hold values from 0 to 191, as said below
- counts: int32 [32], P('seq'), may hold values from 1 to 48, 768 in all
- cotangent: bfloat16 [6144, 8192], P('seq', 'tp'), may hold values from -0.59765625 to 0.59765625
Outputs:
- outgoing_residual: bfloat16 [6144, 8192], P('seq', 'tp')
- attention_output_grad: bfloat16 [1536, 8192], P(None, 'seq')
- adapter_down_gradient: float32 [8192, 64], P('seq')
- adapter_up_gradient: float32 [64, 8192], P(None, 'tp')
- router_gate_gradient: float32 [1536], P('seq')
The draws below stay inside these ranges and needn't reach their ends.
Inputs may be any that keep to these rules, and one draw needn't show every extreme that they name: `counts`: every shard has at least one live slot, all shards together have 768, and some shard has all 48 slots live. `selected`: within each shard's 48 slots the entries are distinct token positions of that shard; only the first counts entries of a shard are live.
All inputs are finite; a program needn't handle non-finite values.
Results may differ from the reference program's by a relative error of at most 0.0058.
Values may be sent and summed in bfloat16 or wider, within the bound.
A program may use at most 64 MiB of HBM per device.

```python
import math
import jax
import jax.numpy as jnp
import numpy as np
from jax import lax

MODEL_WIDTH = 8192
ADAPTER_RANK = 64
QBLOCK = 64
TOK_DEV = 192
HEAD_WIDTH_TOTAL = 8192
CAP = 48
TOKENS = 6144
SELECTED = 768
SLOTS = 1536
N_SEQ = 32


def draw_selected(key, part):
    shard_keys = jax.random.split(key, TOKENS // TOK_DEV)

    def one_shard(shard_key):
        return jax.random.permutation(shard_key, TOK_DEV)[:CAP]
    return jax.vmap(one_shard)(shard_keys).reshape(-1).astype(jnp.int32)


def with_ends(array, rng, least, largest):
    longest = array.shape.index(max(array.shape))
    spots = []
    for shift in (0, 1):
        where = [jax.random.randint(jax.random.fold_in(rng, axis), (), 0, length) for axis, length in enumerate(array.shape)]
        where[longest] = (where[longest] + shift) % array.shape[longest]
        spots.append(tuple(where))
    return array.at[spots[0]].set(least).at[spots[1]].set(largest)


def levels(own_key, dims, pieces, smallest, largest):
    loudness, own = 1.0, jax.random.fold_in(own_key, 6)
    for dim, parts in pieces:
        heights = jnp.exp(jax.random.uniform(jax.random.fold_in(own, dim), (parts,), jnp.float32, smallest / len(pieces), largest / len(pieces)))
        loudness = loudness * jnp.repeat(heights, dims[dim] // parts).reshape([-1 if axis == dim else 1 for axis in range(len(dims))])
    return loudness


def profile(count, total, reach, slope):
    weights = [(1 << 20) // math.isqrt(rank ** slope) + 1 for rank in range(2, count + 1)]
    surplus, given = total - reach - (count - 1), [1] * (count - 1)
    while surplus > 0:
        candidates = [i for i in range(count - 1) if given[i] < reach]
        whole, left = sum([weights[i] for i in candidates]), surplus
        for i in candidates:
            extra = min(reach - given[i], max(1, left * weights[i] // whole), surplus)
            given[i] = given[i] + extra
            surplus = surplus - extra
    return np.array([reach] + given)


def ragged_sizes(stream_key, amount, total, reach, slope):
    if amount == 2:
        one = jax.random.randint(stream_key, (), max(1, total - reach), min(reach, total - 1) + 1)
        return jnp.stack([one, total - one])
    sizes = jnp.asarray(profile(amount, total, reach, slope), jnp.int32)
    couples = (amount - 1) // 2
    donor, taker = sizes[1:1 + 2 * couples:2], sizes[2:2 + 2 * couples:2]
    room = jnp.minimum(donor - 1, reach - taker)
    shifted = jax.random.randint(jax.random.fold_in(stream_key, 1), (couples,), 0, 1 << 20) % (room + 1)
    sizes = sizes.at[1:1 + 2 * couples:2].set(donor - shifted).at[2:2 + 2 * couples:2].set(taker + shifted)
    return sizes[jax.random.permutation(jax.random.fold_in(stream_key, 2), amount)]


def centred(key, shape, scale, most, cuts=(), kind=jnp.bfloat16):
    drawn = jax.random.normal(key, shape, jnp.float32) * scale
    if len(cuts) > 0:
        drawn = levels(key, shape, cuts, -0.22, 0.18) * drawn
    return jnp.clip(drawn, min=-most, max=most).astype(kind)


def setup_inputs(seed: int = 0) -> dict:
    key_of = jax.random.split(jax.random.key(seed), 11)
    return {
        "residual": centred(key_of[0], (TOKENS, MODEL_WIDTH), 1.0, 6.0, ((0, 32), (1, 16))),
        "attention": centred(key_of[1], (SLOTS, HEAD_WIDTH_TOTAL), 1.0, 6.0, ((0, 32),)),
        "quantized_codes": with_ends(jax.random.randint(key_of[2], (HEAD_WIDTH_TOTAL, MODEL_WIDTH), 0, 16), jax.random.fold_in(key_of[2], 1), 0, 15).astype(jnp.int32),
        "absmax": jnp.clip(jnp.exp(math.log(0.05) - 2.3025851 * jax.random.uniform(key_of[3], (HEAD_WIDTH_TOTAL, MODEL_WIDTH // QBLOCK), jnp.float32) ** levels(key_of[3], (HEAD_WIDTH_TOTAL, MODEL_WIDTH // QBLOCK), ((0, 32), (1, 16)), -0.2, 0.2)), 0.005, 0.05),
        "adapter_down": centred(key_of[4], (HEAD_WIDTH_TOTAL, ADAPTER_RANK), HEAD_WIDTH_TOTAL ** -0.5, 0.0625, ((0, 32),)),
        "adapter_up": centred(key_of[5], (ADAPTER_RANK, MODEL_WIDTH), ADAPTER_RANK ** -0.5, 0.75, ((1, 16),)),
        "routed_slot_gate": jnp.clip(0.2 + 0.8 * jax.random.uniform(key_of[6], (SLOTS,), jnp.float32) ** levels(key_of[6], (SLOTS,), ((0, 32),), -0.2, 0.2), 0.2, 1.0),
        "selected": draw_selected(jax.random.fold_in(key_of[10], 71), 0),
        "counts": ragged_sizes(key_of[8], N_SEQ, SELECTED, CAP, 2).astype(jnp.int32),
        "cotangent": centred(key_of[9], (TOKENS, MODEL_WIDTH), 0.1, 0.59765625, ((0, 32), (1, 16))),
    }


LEVELS = (-1.0, -0.6961928009986877, -0.5250730514526367, -0.39491748809814453,
          -0.28444138169288635, -0.18477343022823334, -0.09105003625154495, 0.0,
          0.07958029955625534, 0.16093020141124725, 0.24611230194568634, 0.33791524171829224,
          0.44070982933044434, 0.5626170039176941, 0.7229568362236023, 1.0)
adapter_scale = 0.25


def precise_matmul(left, right):
    return jnp.dot(left, right, precision=lax.Precision.HIGHEST, preferred_element_type=jnp.float32)


def reference(residual, attention, quantized_codes, absmax, adapter_down, adapter_up, routed_slot_gate, selected, counts, cotangent):
    lookup = jnp.asarray(LEVELS, jnp.float32)
    scales = jnp.repeat(absmax, QBLOCK, axis=1)
    projection_weight = (lookup[quantized_codes] * scales).astype(jnp.bfloat16)
    adapter_product = jnp.dot(attention, adapter_down, preferred_element_type=jnp.float32)
    block_output = jnp.dot(attention, projection_weight, preferred_element_type=jnp.float32) + adapter_scale * precise_matmul(adapter_product, adapter_up.astype(jnp.float32))
    slot_ids = jnp.arange(SLOTS, dtype=jnp.int32)
    shard_ids = slot_ids // CAP
    live_slot = (slot_ids % CAP) < counts[shard_ids]
    token = (shard_ids * TOK_DEV + selected).astype(jnp.int32)
    target = jnp.where(live_slot, token, TOKENS).astype(jnp.int32)
    picked = residual[token].astype(jnp.float32)
    updated = (picked + routed_slot_gate[:, None] * block_output).astype(jnp.bfloat16)
    outgoing_residual = residual.at[target].set(updated, mode="drop")
    upstream = jnp.where(live_slot[:, None], cotangent[token].astype(jnp.float32), 0.0)
    router_gate_gradient = jnp.sum(upstream * block_output, axis=1)
    output_gradient = (routed_slot_gate[:, None] * upstream).astype(jnp.bfloat16)
    adapter_rank_gradient = (adapter_scale * jnp.dot(output_gradient, adapter_up.T, preferred_element_type=jnp.float32)).astype(jnp.bfloat16)
    attention_output_grad = (jnp.dot(output_gradient, projection_weight.T, preferred_element_type=jnp.float32)
                 + jnp.dot(adapter_rank_gradient, adapter_down.T, preferred_element_type=jnp.float32)).astype(jnp.bfloat16)
    adapter_down_gradient = jnp.dot(attention.T, adapter_rank_gradient, preferred_element_type=jnp.float32)
    adapter_up_gradient = adapter_scale * precise_matmul(adapter_product.T, output_gradient.astype(jnp.float32))
    return outgoing_residual, attention_output_grad, adapter_down_gradient, adapter_up_gradient, router_gate_gradient
```

```python
import functools

import jax
import jax.numpy as jnp
from jax import lax
from jax.experimental import pallas as pl
from jax.experimental.pallas import tpu as pltpu
from jax.sharding import PartitionSpec as P

LEVELS = (
    -1.0,
    -0.6961928009986877,
    -0.5250730514526367,
    -0.39491748809814453,
    -0.28444138169288635,
    -0.18477343022823334,
    -0.09105003625154495,
    0.0,
    0.07958029955625534,
    0.16093020141124725,
    0.24611230194568634,
    0.33791524171829224,
    0.44070982933044434,
    0.5626170039176941,
    0.7229568362236023,
    1.0,
)
adapter_scale = 0.25
F32, BF16 = jnp.float32, jnp.bfloat16
MESH = pl.DeviceIdType.MESH

NX, NZ, NY, NC = 4, 8, 8, 2

(S_G, S_W, S_DT, S_A, S_ASIB, S_RSIB, S_RRS, S_RAG, S_HSIB, S_HRS, S_FX, S_FY, S_FSIB,
 S_URS, S_UX, S_UAG, S_ORS, S_DX, S_GG, S_FX2, N_SEM) = range(21)
(L_COT, L_CODES, L_ABS, L_DOWN, L_UP, L_RES, L_A, L_FOUT, L_OUT, L_D, L_U, N_LOC) = range(12)


def dot(a, b, ca, cb):
    return lax.dot_general(a, b, (((ca,), (cb,)), ((), ())), preferred_element_type=F32)


def split(value):
    high = value.astype(BF16)
    return high, (value - high.astype(F32)).astype(BF16)


def to_column(row, n):
    at = lax.broadcasted_iota(jnp.int32, (n, n), 0) == lax.broadcasted_iota(jnp.int32, (n, n), 1)
    return jnp.sum(jnp.where(at, jnp.broadcast_to(row, (n, n)), 0.0), axis=1, keepdims=True)


def to_row(column, n):
    at = lax.broadcasted_iota(jnp.int32, (n, n), 0) == lax.broadcasted_iota(jnp.int32, (n, n), 1)
    return jnp.sum(jnp.where(at, jnp.broadcast_to(column, (n, n)), 0.0), axis=0, keepdims=True)


def kernel(nx, nz, ny,
           res_hbm, attn, codes_hbm, abs_hbm, down_hbm, up_hbm, gate_ref, sel_ref, counts_ref, cot_hbm,
           out_res, out_ag, out_d, out_u, out_gate,
           res, codes, absm, up, cot, scales,
           a_all, w_all, dt_all, g_all,
           rt, rt_sib, rt_send, rt_recv, rag_send, rag,
           h_send, h_sib, hs, hr, f_send, fx,
           u_send, u_recv, ux_send, ux_recv, uag,
           o_send, o_recv, o_home, new_res,
           d_send, d_recv, d_new, u_new, gg_send, gg_recv,
           ssem, rsem, lsem):
    tokens, cols = res.shape
    heads = w_all.shape[1]
    cap = gate_ref.shape[1]
    rank = up.shape[0]
    slots = nz * cap
    hx = nx // NC
    ntp = ny * NC

    seq = lax.axis_index("seq")
    tp = lax.axis_index("tp")
    x, z = seq // nz, seq % nz
    y, c = tp // NC, tp % NC

    def dev_x(k):
        return (((x + k) % nx) * nz + z, tp)

    def dev_z(k):
        return (x * nz + (z + k) % nz, tp)

    def dev_y(k):
        return (seq, ((y + k) % ny) * NC + c)

    def dev_tp(k):
        return (seq, (tp + k) % ntp)

    sibling = (seq, y * NC + (1 - c))

    def send(group, src, dst, device):
        pltpu.make_async_remote_copy(
            src_ref=src, dst_ref=dst, send_sem=ssem.at[group], recv_sem=rsem.at[group],
            device_id=device, device_id_type=MESH,
        ).start()

    def take(group, like):
        pltpu.make_async_copy(like, like, rsem.at[group]).wait()

    def sent(group, like):
        pltpu.make_async_copy(like, like, ssem.at[group]).wait()

    def local(which, src, dst):
        copy = pltpu.make_async_copy(src, dst, lsem.at[which])
        copy.start()
        return copy

    cot_in = local(L_COT, cot_hbm, cot)
    codes_in = local(L_CODES, codes_hbm, codes)
    abs_in = local(L_ABS, abs_hbm, absm)
    down_in = local(L_DOWN, down_hbm, dt_all.at[0])
    up_in = local(L_UP, up_hbm, up)
    res_in = local(L_RES, res_hbm, res)

    barrier = pltpu.get_barrier_semaphore()
    for k in range(1, nx):
        pl.semaphore_signal(barrier, inc=1, device_id=dev_x(k), device_id_type=MESH)
    for k in range(1, nz):
        pl.semaphore_signal(barrier, inc=1, device_id=dev_z(k), device_id_type=MESH)
    for k in range(1, ntp):
        pl.semaphore_signal(barrier, inc=1, device_id=dev_tp(k), device_id_type=MESH)

    for i in range(nx):
        at = pl.multiple_of((((x + i) % nx) * nz + z) * heads, heads)
        local(L_A, attn.at[:, pl.ds(at, heads)], a_all.at[i, pl.ds(0, cap)])

    gate = to_column(gate_ref[...], cap)
    picked_token = to_column(sel_ref[...].astype(F32), cap)
    live = lax.broadcasted_iota(jnp.int32, (cap, tokens), 0) < counts_ref[...]
    pick = jnp.where(
        live & (lax.broadcasted_iota(jnp.int32, (cap, tokens), 1).astype(F32) == picked_token), 1.0, 0.0)
    pick_bf = pick.astype(BF16)
    cot_in.wait()
    upstream = dot(pick_bf, cot[...], 1, 0)
    g_all[pl.ds(0, cap), :] = (gate * upstream).astype(BF16)

    codes_in.wait()
    abs_in.wait()
    step = 32

    scale_high = absm[...].astype(BF16)
    rest = absm[...] - scale_high.astype(F32)
    scale_mid, scale_low = split(rest)
    qblocks = absm.shape[0]
    spread_to = jnp.where(
        lax.broadcasted_iota(jnp.int32, (qblocks, cols), 1) // (cols // qblocks)
        == lax.broadcasted_iota(jnp.int32, (qblocks, cols), 0), 1.0, 0.0).astype(BF16)
    scales[...] = (dot(scale_high, spread_to, 0, 0) + dot(scale_mid, spread_to, 0, 0)
                   + dot(scale_low, spread_to, 0, 0))

    def dequantize(n, carry):
        rows = pl.ds(pl.multiple_of(n * step, step), step)
        for q in range(cols // 128):
            code = codes[rows, pl.ds(q * 128, 128)]
            b0, b1, b2, b3 = [(code & (1 << bit)) != 0 for bit in range(4)]
            level = LEVELS
            for bit in (b0, b1, b2, b3):
                level = [jnp.where(bit, level[m + 1], level[m]) for m in range(0, len(level), 2)]
            scale = scales[rows, pl.ds(q * 128, 128)]
            w_all[0, rows, pl.ds(q * 128, 128)] = (level[0] * scale).astype(BF16)
        return carry

    lax.fori_loop(0, heads // step, dequantize, 0)
    down_in.wait()

    pl.semaphore_wait(barrier, (nx - 1) + (nz - 1) + (ntp - 1))

    for k in range(1, nz):
        send(S_G, g_all.at[pl.ds(0, cap)], g_all.at[pl.ds(cap * (nz - k), cap)], dev_z(k))
    for k in range(1, nx):
        send(S_W, w_all.at[0], w_all.at[nx - k], dev_x(k))
        send(S_DT, dt_all.at[0], dt_all.at[nx - k], dev_x(k))
    for k in range(1, nz):
        for n in range(hx):
            i = hx * c + n
            at = pl.multiple_of((((x + i) % nx) * nz + (z + k) % nz) * heads, heads)
            send(S_A, attn.at[:, pl.ds(at, heads)],
                 a_all.at[i, pl.ds(cap * (nz - k), cap)], dev_z(k))

    g_rest = g_all.at[pl.ds(cap, slots - cap)]
    w_rest = w_all.at[pl.ds(1, nx - 1)]
    dt_rest = dt_all.at[pl.ds(1, nx - 1)]
    a_mine = a_all.at[pl.ds(hx * c, hx), pl.ds(cap, slots - cap)]
    a_other = a_all.at[pl.ds(hx * (1 - c), hx), pl.ds(cap, slots - cap)]

    up_in.wait()
    take(S_G, g_rest)
    rt[...] = adapter_scale * dot(up[...], g_all[...], 1, 1)
    send(S_RSIB, rt, rt_sib, sibling)
    rank_part = (adapter_scale * dot(g_all[...], up[...], 1, 1)).astype(BF16)

    take(S_W, w_rest)
    take(S_DT, dt_rest)
    for i in range(nx):
        part = dot(g_all[...], w_all[i], 1, 1) + dot(rank_part, dt_all[i], 1, 0)
        for j in range(nz):
            h_send[i // hx, j, i % hx] = part[j * cap:(j + 1) * cap].astype(BF16)
    send(S_HSIB, h_send.at[1 - c], h_sib, sibling)

    take(S_RSIB, rt_sib)
    for j in range(ny):
        rows = pl.ds(j * (rank // ny), rank // ny)
        rt_send[j] = rt[rows, :] + rt_sib[rows, :]
    for k in range(1, ny):
        send(S_RRS, rt_send.at[(y + k) % ny], rt_recv.at[ny - k], dev_y(k))

    take(S_HSIB, h_sib)
    for j in range(nz):
        hs[j] = (h_send[c, j].astype(F32) + h_sib[j].astype(F32)).astype(BF16)
    for k in range(1, ny):
        send(S_HRS, hs.at[(y + k) % ny], hr.at[ny - k], dev_y(k))

    take(S_RRS, rt_recv.at[pl.ds(1, ny - 1)])
    total = rt_send[y]
    for k in range(1, ny):
        total = total + rt_recv[k]
    rag_send[...] = total.astype(BF16).astype(F32)
    rag[y] = rag_send[...]
    for k in range(1, ny):
        send(S_RAG, rag_send, rag.at[y], dev_y(k))

    take(S_A, a_mine)
    send(S_ASIB, a_mine, a_mine, sibling)
    a_home = a_all.at[:, pl.ds(0, cap)]
    pltpu.make_async_copy(a_home, a_home, lsem.at[L_A]).wait()
    take(S_ASIB, a_other)

    low = jnp.zeros((slots, rank), F32)
    low_t = jnp.zeros((rank, slots), F32)
    for i in range(nx):
        low = low + dot(a_all[i], dt_all[i], 1, 1)
        low_t = low_t + dot(dt_all[i], a_all[i], 1, 1)
    t_high, t_low = split(low_t)
    part = adapter_scale * (dot(t_high, g_all[...], 1, 0) + dot(t_low, g_all[...], 1, 0))
    for j in range(nz):
        u_send[j] = part[j * (rank // nz):(j + 1) * (rank // nz)]
    for k in range(1, nz):
        send(S_URS, u_send.at[(z + k) % nz], u_recv.at[nz - k], dev_z(k))

    high, small = split(adapter_scale * low)
    part = dot(high, up[...], 1, 0) + dot(small, up[...], 1, 0)
    for i in range(nx):
        part = part + dot(a_all[i], w_all[i], 1, 0)
    o_home[...] = part[:cap]
    for j in range(1, nz):
        o_send[j] = part[j * cap:(j + 1) * cap].astype(BF16)
    for k in range(1, nz):
        send(S_ORS, o_send.at[k], o_recv.at[nz - k], dev_z(k))

    take(S_HRS, hr.at[pl.ds(1, ny - 1)])
    total = hs[y].astype(F32)
    for k in range(1, ny):
        total = total + hr[k].astype(F32)
    f_send[...] = total.astype(BF16)
    shard_z = (z + y) % nz
    for n in range(hx):
        i = hx * c + n
        if n == 0:
            @pl.when(c == 0)
            def _():
                fx[0] = f_send[0]

            @pl.when(c != 0)
            def _():
                send(S_FX, f_send.at[0], fx.at[0], dev_x(hx))
        else:
            send(S_FX2 + n - 1, f_send.at[n], fx.at[n], dev_x(i))

    take(S_RAG, rag.at[pl.ds(0, ny - 1)])
    full_rt = jnp.reshape(rag[...], (rank, slots)).astype(BF16)
    for i in range(nx):
        d_send[i] = dot(full_rt, a_all[i], 1, 0)
    for k in range(1, nx):
        send(S_DX, d_send.at[k], d_recv.at[nx - k], dev_x(k))

    for n in range(hx):
        if n == 0:
            @pl.when(c != 0)
            def _():
                take(S_FX, fx.at[0])
        else:
            take(S_FX2 + n - 1, fx.at[n])
    for n in range(hx):
        row = (x + nx - (hx * c + n)) % nx
        local(L_FOUT, fx.at[n], out_ag.at[row, shard_z])
        for k in range(1, ny):
            send(S_FY, fx.at[n], out_ag.at[row, shard_z], dev_y(k))

    take(S_URS, u_recv.at[pl.ds(1, nz - 1)])
    total = u_send[z]
    for k in range(1, nz):
        total = total + u_recv[k]
    ux_send[...] = total
    for k in range(1, nx):
        send(S_UX, ux_send, ux_recv.at[nx - k], dev_x(k))

    take(S_ORS, o_recv.at[pl.ds(1, nz - 1)])
    block = o_home[...]
    for k in range(1, nz):
        block = block + o_recv[k].astype(F32)
    res_in.wait()
    gate_part = to_row(jnp.sum(upstream * block, axis=1, keepdims=True), cap)
    gg_send[...] = jnp.zeros_like(gg_send)
    gg_send[:, pl.ds(0, cap)] = jnp.broadcast_to(gate_part, (8, cap))
    for k in range(1, ntp):
        send(S_GG, gg_send, gg_recv.at[ntp - k], dev_tp(k))
    picked = dot(pick_bf, res[...], 1, 0)
    updated = (picked + gate * block).astype(BF16)
    spread = dot(pick_bf, updated, 0, 0)
    taken = dot(pick_bf, jnp.ones((cap, 128), BF16), 0, 0)[:, :1] > 0.5
    new_res[...] = jnp.where(taken, spread, res[...].astype(F32)).astype(BF16)
    out_copy = local(L_OUT, new_res, out_res)

    take(S_UX, ux_recv.at[pl.ds(1, nx - 1)])
    total = ux_send[...]
    for k in range(1, nx):
        total = total + ux_recv[k]
    ux_send_sum = total
    sent(S_UX, ux_recv.at[pl.ds(1, nx - 1)])
    ux_send[...] = ux_send_sum
    uag[z] = ux_send_sum
    for k in range(1, nz):
        send(S_UAG, ux_send, uag.at[z], dev_z(k))

    take(S_DX, d_recv.at[pl.ds(1, nx - 1)])
    total = d_send[0]
    for k in range(1, nx):
        total = total + d_recv[k]
    d_new[...] = total
    d_copy = local(L_D, d_new, out_d)

    take(S_FY, out_ag.at[pl.ds(0, hx), pl.ds(0, ny - 1)])
    pltpu.make_async_copy(fx, fx, lsem.at[L_FOUT]).wait()
    for n in range(hx):
        row = (x + nx - (hx * c + n)) % nx
        send(S_FSIB, out_ag.at[row], out_ag.at[row], sibling)

    take(S_GG, gg_recv.at[pl.ds(1, ntp - 1)])
    total = gg_send[...]
    for k in range(1, ntp):
        total = total + gg_recv[k]
    out_gate[...] = total[:1, :cap]

    take(S_UAG, uag.at[pl.ds(0, nz - 1)])
    u_new[...] = jnp.reshape(uag[...], (rank, cols))
    u_copy = local(L_U, u_new, out_u)
    take(S_FSIB, out_ag.at[pl.ds(0, hx)])

    out_copy.wait()
    d_copy.wait()
    u_copy.wait()
    sent(S_G, g_rest)
    sent(S_W, w_rest)
    sent(S_DT, dt_rest)
    sent(S_A, a_mine)
    sent(S_ASIB, a_mine)
    sent(S_RSIB, rt)
    sent(S_RRS, rt_recv.at[pl.ds(1, ny - 1)])
    sent(S_RAG, rag.at[pl.ds(0, ny - 1)])
    sent(S_HSIB, h_sib)
    sent(S_HRS, hr.at[pl.ds(1, ny - 1)])
    for n in range(hx):
        if n == 0:
            @pl.when(c != 0)
            def _():
                sent(S_FX, fx.at[0])
        else:
            sent(S_FX2 + n - 1, fx.at[n])
    sent(S_FY, out_ag.at[pl.ds(0, hx), pl.ds(0, ny - 1)])
    sent(S_FSIB, out_ag.at[pl.ds(0, hx)])
    sent(S_URS, u_recv.at[pl.ds(1, nz - 1)])
    sent(S_UAG, uag.at[pl.ds(0, nz - 1)])
    sent(S_ORS, o_recv.at[pl.ds(1, nz - 1)])
    sent(S_DX, d_recv.at[pl.ds(1, nx - 1)])
    sent(S_GG, gg_recv.at[pl.ds(1, ntp - 1)])


def body(residual, attention, codes, absmax, down, up, gate, selected, counts, cotangent,
         nx=NX, nz=NZ, ny=NY):
    tokens, cols = residual.shape
    cap = attention.shape[0]
    heads, rank = down.shape
    slots = nz * cap
    hx = nx // NC
    ntp = ny * NC
    anywhere = pl.BlockSpec(memory_space=pl.ANY)
    vmem = pl.BlockSpec(memory_space=pltpu.VMEM)

    def f32(*shape):
        return pltpu.VMEM(shape, F32)

    def bf16(*shape):
        return pltpu.VMEM(shape, BF16)

    outs = pl.pallas_call(
        functools.partial(kernel, nx, nz, ny),
        out_shape=(
            jax.ShapeDtypeStruct((tokens, cols), BF16),
            jax.ShapeDtypeStruct((nx, nz, cap, heads), BF16),
            jax.ShapeDtypeStruct((rank, heads), F32),
            jax.ShapeDtypeStruct((rank, cols), F32),
            jax.ShapeDtypeStruct((1, cap), F32),
        ),
        in_specs=[anywhere] * 6 + [vmem, vmem, vmem, anywhere],
        out_specs=(anywhere, anywhere, anywhere, anywhere, vmem),
        scratch_shapes=[
            bf16(tokens, cols), pltpu.VMEM((heads, cols), jnp.int32), f32(*absmax.shape[::-1]),
            bf16(rank, cols), bf16(tokens, cols), f32(heads, cols),
            bf16(nx, slots, heads), bf16(nx, heads, cols), bf16(nx, rank, heads), bf16(slots, cols),
            f32(rank, slots), f32(rank, slots), f32(ny, rank // ny, slots), f32(ny, rank // ny, slots),
            f32(rank // ny, slots), f32(ny, rank // ny, slots),
            bf16(NC, nz, hx, cap, heads), bf16(nz, hx, cap, heads), bf16(nz, hx, cap, heads),
            bf16(ny, hx, cap, heads), bf16(hx, cap, heads), bf16(hx, cap, heads),
            f32(nz, rank // nz, cols), f32(nz, rank // nz, cols), f32(rank // nz, cols),
            f32(nx, rank // nz, cols), f32(nz, rank // nz, cols),
            bf16(nz, cap, cols), bf16(nz, cap, cols), f32(cap, cols), bf16(tokens, cols),
            f32(nx, rank, heads), f32(nx, rank, heads), f32(rank, heads), f32(rank, cols),
            f32(8, 128), f32(ntp, 8, 128),
            pltpu.SemaphoreType.DMA((N_SEM,)), pltpu.SemaphoreType.DMA((N_SEM,)),
            pltpu.SemaphoreType.DMA((N_LOC,)),
        ],
        compiler_params=pltpu.CompilerParams(
            collective_id=0, has_side_effects=True, vmem_limit_bytes=56 << 20),
        name="block_step",
    )(residual, attention, codes, absmax.T, down.T, up, gate.reshape(1, cap), selected.reshape(1, cap),
      counts.reshape(1, 1), cotangent)
    new_res, head_grad, d_grad, u_grad, g_grad = outs
    return new_res, head_grad.reshape(nx * nz * cap, heads), d_grad.T, u_grad, g_grad.reshape(cap)


def solution(mesh):
    return jax.shard_map(
        body,
        mesh=mesh,
        in_specs=(
            P("seq", "tp"),
            P("seq", None),
            P("seq", "tp"),
            P("seq", "tp"),
            P("seq", None),
            P(None, "tp"),
            P("seq"),
            P("seq"),
            P("seq"),
            P("seq", "tp"),
        ),
        out_specs=(P("seq", "tp"), P(None, "seq"), P("seq", None), P(None, "tp"), P("seq")),
        check_vma=False,
    )
```

```python
import functools

import jax
import jax.numpy as jnp
from jax import lax
from jax.experimental import pallas as pl
from jax.experimental.pallas import tpu as pltpu
from jax.sharding import PartitionSpec as P

LEVELS = (
    -1.0,
    -0.6961928009986877,
    -0.5250730514526367,
    -0.39491748809814453,
    -0.28444138169288635,
    -0.18477343022823334,
    -0.09105003625154495,
    0.0,
    0.07958029955625534,
    0.16093020141124725,
    0.24611230194568634,
    0.33791524171829224,
    0.44070982933044434,
    0.5626170039176941,
    0.7229568362236023,
    1.0,
)
adapter_scale = 0.25
F32, BF16 = jnp.float32, jnp.bfloat16
MESH = pl.DeviceIdType.MESH

NX, NZ, NY, NC = 4, 8, 8, 2

(S_G, S_A, S_F0, S_F1, S_AZ, S_W1A, S_W1B, S_W3A, S_W3B, S_W2, S_DT, S_ASIB, S_RSIB, S_RRS, S_RAG,
 S_HSIB, S_HRS, S_FX, S_FSIB, S_URS, S_UX, S_UAG, S_ORS, S_DX, S_GG, N_SEM) = (
    0, 5, 10, 15, 20, *range(22, 32), 32, 34, 36, 38, *range(40, 47))
(L_COT, L_CODES, L_ABS, L_DOWN, L_UP, L_RES, L_A, L_OUT, L_D, L_U, L_FOUT, N_LOC) = (*range(11), 12)


def dot(a, b, ca, cb):
    return lax.dot_general(a, b, (((ca,), (cb,)), ((), ())), preferred_element_type=F32)


def split(value):
    high = value.astype(BF16)
    return high, (value - high.astype(F32)).astype(BF16)


def to_column(row, n):
    at = lax.broadcasted_iota(jnp.int32, (n, n), 0) == lax.broadcasted_iota(jnp.int32, (n, n), 1)
    return jnp.sum(jnp.where(at, jnp.broadcast_to(row, (n, n)), 0.0), axis=1, keepdims=True)


def to_row(column, n):
    at = lax.broadcasted_iota(jnp.int32, (n, n), 0) == lax.broadcasted_iota(jnp.int32, (n, n), 1)
    return jnp.sum(jnp.where(at, jnp.broadcast_to(column, (n, n)), 0.0), axis=0, keepdims=True)


def kernel(nx, nz, ny,
           res_hbm, attn, codes_hbm, abs_hbm, down_hbm, up_hbm, gate_ref, sel_ref, counts_ref, cot_hbm,
           out_res, out_ag, out_d, out_u, out_gate,
           res, codes, absm, up, cot, scales,
           a_all, w_all, dt_all, g_all,
           rt, rt_sib, rt_send, rt_recv, rag_send, rag,
           h_send, h_sib, hs, hr, f_send, fx,
           u_send, u_recv, ux_send, ux_recv, uag,
           o_send, o_recv, o_home, new_res,
           d_send, d_recv, d_new, u_new, gg_send, gg_recv,
           ssem, rsem, lsem):
    tokens, cols = res.shape
    heads = w_all.shape[1]
    cap = gate_ref.shape[1]
    rank = up.shape[0]
    slots = nz * cap
    hx = nx // NC
    ntp = ny * NC

    seq = lax.axis_index("seq")
    tp = lax.axis_index("tp")
    x, z = seq // nz, seq % nz
    y, c = tp // NC, tp % NC

    def dev_x(k):
        return (((x + k) % nx) * nz + z, tp)

    def dev_z(k):
        return (x * nz + (z + k) % nz, tp)

    def dev_y(k):
        return (seq, ((y + k) % ny) * NC + c)

    def dev_tp(k):
        return (seq, (tp + k) % ntp)

    sibling = (seq, y * NC + (1 - c))

    def send(group, src, dst, device):
        pltpu.make_async_remote_copy(
            src_ref=src, dst_ref=dst, send_sem=ssem.at[group], recv_sem=rsem.at[group],
            device_id=device, device_id_type=MESH,
        ).start()

    def take(group, like):
        pltpu.make_async_copy(like, like, rsem.at[group]).wait()

    def sent(group, like):
        pltpu.make_async_copy(like, like, ssem.at[group]).wait()

    def local(which, src, dst):
        copy = pltpu.make_async_copy(src, dst, lsem.at[which])
        copy.start()
        return copy

    def gather_start(group, n, dev, parts):
        for k in sorted({1, n - 1} | ({2, n - 2} if n == 8 else set())):
            which = {n - 1: 0, 1: 1, n - 2: 2, 2: 3}[n - k] if n > 2 else 0
            for src, dst in zip(parts(0, 0), parts(0, k)):
                send(group + which, src, dst, dev(k))

    def gather_forward(group, n, dev, parts, halves, like):
        if n == 2:
            return
        far = n // 2 - 2
        for side, which in ((-1, 2 if far else 0), (1, 3 if far else 1)):
            j = side * (far if far else 1)
            take(group + which, like(1))
            if far:
                for src, dst in zip(parts(j, 0), parts(j, -side)):
                    send(group + 4, src, dst, dev(-side))
            half = 0 if side < 0 else 1
            k = -side * (n // 2 - abs(j))
            for src, dst in zip(halves(j, 0, half), halves(j, k, half)):
                send(group + 4, src, dst, dev(k))

    def gather_finish(group, n, like):
        if n != 4:
            take(group, like(1))
        if n == 8:
            take(group + 1, like(1))
        if n > 2:
            take(group + 4, like(n // 2 - 1))

    def gather_sent(group, n, like):
        for which in range(4 if n == 8 else n // 2):
            sent(group + which, like(1))
        if n > 2:
            sent(group + 4, like(n // 2 - 1))

    def g_parts(j, k):
        return [g_all.at[pl.ds(((j - k) % nz) * cap, cap)]]

    def g_halves(j, k, half):
        return [g_all.at[pl.ds(((j - k) % nz) * cap, cap), pl.ds(half * (cols // 2), cols // 2)]]

    def g_like(n):
        return g_all.at[pl.ds(0, n * cap)]

    def a_part(j, n):
        row = ((y + j + n * (ny // 2)) % nz) * cap
        return a_all.at[hx * c + n, pl.ds(pl.multiple_of(row, cap), cap)]

    def a_parts(j, k):
        return [a_part(j, n) for n in range(hx)]

    def a_halves(j, k, half):
        return [a_part(j, half)]

    def a_like(n):
        return a_all.at[pl.ds(hx * c, hx), pl.ds(0, n * cap)]

    def own(m):
        return jnp.where(c == 0, m, nx - 1 - m)

    def f_row(m):
        return (x + nx - own(m)) % nx

    def f_parts(m):
        return lambda j, k: [fx.at[m] if (j, k) == (0, 0) else out_ag.at[f_row(m), (z + y + j) % nz]]

    def f_halves(m):
        return lambda j, k, half: [
            out_ag.at[f_row(m), (z + y + j) % nz, :, pl.ds(half * (heads // 2), heads // 2)]]

    def f_like(n):
        return out_ag.at[0, pl.ds(0, n)]

    cot_in = local(L_COT, cot_hbm, cot)
    codes_in = local(L_CODES, codes_hbm, codes)
    abs_in = local(L_ABS, abs_hbm, absm)
    down_in = local(L_DOWN, down_hbm, dt_all.at[0])
    up_in = local(L_UP, up_hbm, up)
    res_in = local(L_RES, res_hbm, res)

    barrier = pltpu.get_barrier_semaphore()
    for k in range(1, nx):
        pl.semaphore_signal(barrier, inc=1, device_id=dev_x(k), device_id_type=MESH)
    for k in range(1, nz):
        pl.semaphore_signal(barrier, inc=1, device_id=dev_z(k), device_id_type=MESH)
    for k in range(1, ntp):
        pl.semaphore_signal(barrier, inc=1, device_id=dev_tp(k), device_id_type=MESH)

    gate = to_column(gate_ref[...], cap)
    picked_token = to_column(sel_ref[...].astype(F32), cap)
    live = lax.broadcasted_iota(jnp.int32, (cap, tokens), 0) < counts_ref[...]
    pick = jnp.where(
        live & (lax.broadcasted_iota(jnp.int32, (cap, tokens), 1).astype(F32) == picked_token), 1.0, 0.0)
    pick_bf = pick.astype(BF16)
    cot_in.wait()
    upstream = dot(pick_bf, cot[...], 1, 0)
    g_all[pl.ds(0, cap), :] = (gate * upstream).astype(BF16)

    codes_in.wait()
    abs_in.wait()
    step = 32

    scale_high = absm[...].astype(BF16)
    rest = absm[...] - scale_high.astype(F32)
    scale_mid, scale_low = split(rest)
    qblocks = absm.shape[0]
    spread_to = jnp.where(
        lax.broadcasted_iota(jnp.int32, (qblocks, cols), 1) // (cols // qblocks)
        == lax.broadcasted_iota(jnp.int32, (qblocks, cols), 0), 1.0, 0.0).astype(BF16)
    scales[...] = (dot(scale_high, spread_to, 0, 0) + dot(scale_mid, spread_to, 0, 0)
                   + dot(scale_low, spread_to, 0, 0))

    def dequantize(n, carry):
        rows = pl.ds(pl.multiple_of(n * step, step), step)
        for q in range(cols // 128):
            code = codes[rows, pl.ds(q * 128, 128)]
            b0, b1, b2, b3 = [(code & (1 << bit)) != 0 for bit in range(4)]
            level = LEVELS
            for bit in (b0, b1, b2, b3):
                level = [jnp.where(bit, level[m + 1], level[m]) for m in range(0, len(level), 2)]
            scale = scales[rows, pl.ds(q * 128, 128)]
            w_all[0, rows, pl.ds(q * 128, 128)] = (level[0] * scale).astype(BF16)
        return carry

    lax.fori_loop(0, heads // step, dequantize, 0)
    down_in.wait()

    pl.semaphore_wait(barrier, (nx - 1) + (nz - 1) + (ntp - 1))

    for n in range(hx):
        off = (y + n * (ny // 2)) % nz
        i = hx * c + n
        dest = (z + nz - off) % nz
        at = pl.multiple_of((((x + i) % nx) * nz + dest) * heads, heads)
        block = attn.at[:, pl.ds(at, heads)]
        place = a_all.at[i, pl.ds(pl.multiple_of(off * cap, cap), cap)]

        @pl.when(off == 0)
        def _():
            local(L_A, block, place)

        @pl.when(off != 0)
        def _():
            send(S_AZ + n, block, place, (x * nz + dest, tp))

    gather_start(S_G, nz, dev_z, g_parts)
    hh = heads // 2
    first, second = pl.ds(0, hh), pl.ds(hh, hh)
    send(S_W3A, w_all.at[0, first], w_all.at[3, first], dev_x(1))
    send(S_W1A, w_all.at[0, second], w_all.at[1, second], dev_x(3))
    for k in range(1, nx):
        send(S_DT, dt_all.at[0], dt_all.at[nx - k], dev_x(k))
    send(S_W3B, w_all.at[0, second], w_all.at[3, second], dev_x(1))
    send(S_W1B, w_all.at[0, first], w_all.at[1, first], dev_x(3))

    for n in range(hx):
        off = (y + n * (ny // 2)) % nz

        @pl.when(off == 0)
        def _():
            place = a_all.at[0, pl.ds(0, cap)]
            pltpu.make_async_copy(place, place, lsem.at[L_A]).wait()

        @pl.when(off != 0)
        def _():
            take(S_AZ + n, a_all.at[0, pl.ds(0, cap)])
    gather_start(S_A, ny, dev_y, a_parts)
    gather_forward(S_G, nz, dev_z, g_parts, g_halves, g_like)
    half_w = w_all.at[0, first]
    take(S_W3A, half_w)
    send(S_W2, w_all.at[3, first], w_all.at[2, first], dev_x(1))
    take(S_W1A, half_w)
    send(S_W2, w_all.at[1, second], w_all.at[2, second], dev_x(3))
    gather_forward(S_A, ny, dev_y, a_parts, a_halves, a_like)

    up_in.wait()
    gather_finish(S_G, nz, g_like)
    rank_part = (adapter_scale * dot(g_all[...], up[...], 1, 1)).astype(BF16)

    def head_block(i):
        part = dot(g_all[...], w_all[i], 1, 1) + dot(rank_part, dt_all[i], 1, 0)
        for j in range(nz):
            h_send[i, j] = part[j * cap:(j + 1) * cap].astype(BF16)

    def head_pair(m):
        send(S_HSIB + m, h_send.at[nx - 1 - own(m)], h_sib.at[m], sibling)

    def head_sum(m):
        take(S_HSIB + m, h_sib.at[m])
        for j in range(nz):
            hs[m, j] = (h_send[own(m), j].astype(F32) + h_sib[m, j].astype(F32)).astype(BF16)
        for k in range(1, ny):
            send(S_HRS + m, hs.at[m, (y + k) % ny], hr.at[m, ny - k], dev_y(k))

    def head_home(m):
        take(S_HRS + m, hr.at[m, pl.ds(1, ny - 1)])
        total = hs[m, y].astype(F32)
        for k in range(1, ny):
            total = total + hr[m, k].astype(F32)
        f_send[m] = total.astype(BF16)
        if m == 0:
            @pl.when(c == 0)
            def _():
                fx[0] = f_send[0]

            @pl.when(c != 0)
            def _():
                send(S_FX, f_send.at[0], fx.at[0], dev_x(nx - 1))
        else:
            send(S_FX + m, f_send.at[m], fx.at[m], dev_x(own(m)))

    def head_gather(m):
        if m == 0:
            @pl.when(c != 0)
            def _():
                take(S_FX, fx.at[0])
        else:
            take(S_FX + m, fx.at[m])
        local(L_FOUT + m, fx.at[m], out_ag.at[f_row(m), shard_z])
        gather_start(S_F0 + 5 * m, ny, dev_y, f_parts(m))

    def head_forward(m):
        gather_forward(S_F0 + 5 * m, ny, dev_y, f_parts(m), f_halves(m), f_like)

    def head_finish(m):
        gather_finish(S_F0 + 5 * m, ny, f_like)
        pltpu.make_async_copy(fx.at[m], fx.at[m], lsem.at[L_FOUT + m]).wait()
        send(S_FSIB + m, out_ag.at[f_row(m)], out_ag.at[f_row(m)], sibling)

    shard_z = (z + y) % nz
    take(S_DT, dt_all.at[pl.ds(1, nx - 1)])
    head_block(0)
    take(S_W3B, half_w)
    head_block(3)
    head_pair(0)
    rt[...] = adapter_scale * dot(up[...], g_all[...], 1, 1)
    send(S_RSIB, rt, rt_sib, sibling)
    take(S_W1B, half_w)
    head_block(1)
    head_sum(0)
    take(S_W2, w_all.at[0])
    head_block(2)
    head_pair(1)
    gather_finish(S_A, ny, a_like)
    a_mine = a_all.at[pl.ds(hx * c, hx)]
    send(S_ASIB, a_mine, a_mine, sibling)
    take(S_RSIB, rt_sib)
    for j in range(ny):
        rows = pl.ds(j * (rank // ny), rank // ny)
        rt_send[j] = rt[rows, :] + rt_sib[rows, :]
    for k in range(1, ny):
        send(S_RRS, rt_send.at[(y + k) % ny], rt_recv.at[ny - k], dev_y(k))
    head_sum(1)

    take(S_ASIB, a_mine)
    low = jnp.zeros((slots, rank), F32)
    low_t = jnp.zeros((rank, slots), F32)
    for i in range(nx):
        low = low + dot(a_all[i], dt_all[i], 1, 1)
        low_t = low_t + dot(dt_all[i], a_all[i], 1, 1)
    t_high, t_low = split(low_t)
    part = adapter_scale * (dot(t_high, g_all[...], 1, 0) + dot(t_low, g_all[...], 1, 0))
    for j in range(nz):
        u_send[j] = part[j * (rank // nz):(j + 1) * (rank // nz)]
    for k in range(1, nz):
        send(S_URS, u_send.at[(z + k) % nz], u_recv.at[nz - k], dev_z(k))

    high, small = split(adapter_scale * low)
    part = dot(high, up[...], 1, 0) + dot(small, up[...], 1, 0)
    for i in range(nx):
        part = part + dot(a_all[i], w_all[i], 1, 0)
    o_home[...] = part[:cap]
    for j in range(1, nz):
        o_send[j] = part[j * cap:(j + 1) * cap].astype(BF16)
    for k in range(1, nz):
        send(S_ORS, o_send.at[k], o_recv.at[nz - k], dev_z(k))

    take(S_RRS, rt_recv.at[pl.ds(1, ny - 1)])
    total = rt_send[y]
    for k in range(1, ny):
        total = total + rt_recv[k]
    rag_send[...] = total.astype(BF16).astype(F32)
    rag[y] = rag_send[...]
    for k in range(1, ny):
        send(S_RAG, rag_send, rag.at[y], dev_y(k))

    head_home(0)
    head_home(1)
    head_gather(0)

    take(S_RAG, rag.at[pl.ds(0, ny - 1)])
    full_rt = jnp.reshape(rag[...], (rank, slots)).astype(BF16)
    for i in range(nx):
        d_send[i] = dot(full_rt, a_all[i], 1, 0)
    for k in range(1, nx):
        send(S_DX, d_send.at[k], d_recv.at[nx - k], dev_x(k))
    head_gather(1)
    head_forward(0)

    take(S_URS, u_recv.at[pl.ds(1, nz - 1)])
    total = u_send[z]
    for k in range(1, nz):
        total = total + u_recv[k]
    ux_send[...] = total
    for k in range(1, nx):
        send(S_UX, ux_send, ux_recv.at[nx - k], dev_x(k))

    head_forward(1)
    take(S_ORS, o_recv.at[pl.ds(1, nz - 1)])
    block = o_home[...]
    for k in range(1, nz):
        block = block + o_recv[k].astype(F32)
    res_in.wait()
    gate_part = to_row(jnp.sum(upstream * block, axis=1, keepdims=True), cap)
    gg_send[...] = jnp.zeros_like(gg_send)
    gg_send[:, pl.ds(0, cap)] = jnp.broadcast_to(gate_part, (8, cap))
    for k in range(1, ntp):
        send(S_GG, gg_send, gg_recv.at[ntp - k], dev_tp(k))
    picked = dot(pick_bf, res[...], 1, 0)
    updated = (picked + gate * block).astype(BF16)
    spread = dot(pick_bf, updated, 0, 0)
    taken = dot(pick_bf, jnp.ones((cap, 128), BF16), 0, 0)[:, :1] > 0.5
    new_res[...] = jnp.where(taken, spread, res[...].astype(F32)).astype(BF16)
    out_copy = local(L_OUT, new_res, out_res)

    take(S_UX, ux_recv.at[pl.ds(1, nx - 1)])
    total = ux_send[...]
    for k in range(1, nx):
        total = total + ux_recv[k]
    ux_send_sum = total
    sent(S_UX, ux_recv.at[pl.ds(1, nx - 1)])
    ux_send[...] = ux_send_sum
    uag[z] = ux_send_sum
    for k in range(1, nz):
        send(S_UAG, ux_send, uag.at[z], dev_z(k))

    take(S_DX, d_recv.at[pl.ds(1, nx - 1)])
    total = d_send[0]
    for k in range(1, nx):
        total = total + d_recv[k]
    d_new[...] = total
    d_copy = local(L_D, d_new, out_d)

    for m in range(hx):
        head_finish(m)

    take(S_GG, gg_recv.at[pl.ds(1, ntp - 1)])
    total = gg_send[...]
    for k in range(1, ntp):
        total = total + gg_recv[k]
    out_gate[...] = total[:1, :cap]

    take(S_UAG, uag.at[pl.ds(0, nz - 1)])
    u_new[...] = jnp.reshape(uag[...], (rank, cols))
    u_copy = local(L_U, u_new, out_u)
    for m in range(hx):
        take(S_FSIB + m, out_ag.at[0])

    out_copy.wait()
    d_copy.wait()
    u_copy.wait()
    for n in range(hx):
        @pl.when((y + n * (ny // 2)) % nz != 0)
        def _():
            sent(S_AZ + n, a_all.at[0, pl.ds(0, cap)])
    gather_sent(S_G, nz, g_like)
    gather_sent(S_A, ny, a_like)
    for m in range(hx):
        gather_sent(S_F0 + 5 * m, ny, f_like)
    for group in (S_W1A, S_W1B, S_W3A, S_W3B):
        sent(group, half_w)
    sent(S_W2, w_all.at[0])
    sent(S_DT, dt_all.at[pl.ds(1, nx - 1)])
    sent(S_ASIB, a_mine)
    sent(S_RSIB, rt)
    sent(S_RRS, rt_recv.at[pl.ds(1, ny - 1)])
    sent(S_RAG, rag.at[pl.ds(0, ny - 1)])
    for m in range(hx):
        sent(S_HSIB + m, h_sib.at[m])
        sent(S_HRS + m, hr.at[m, pl.ds(1, ny - 1)])
        sent(S_FSIB + m, out_ag.at[0])

    @pl.when(c != 0)
    def _():
        sent(S_FX, fx.at[0])
    sent(S_FX + 1, fx.at[1])
    sent(S_URS, u_recv.at[pl.ds(1, nz - 1)])
    sent(S_UAG, uag.at[pl.ds(0, nz - 1)])
    sent(S_ORS, o_recv.at[pl.ds(1, nz - 1)])
    sent(S_DX, d_recv.at[pl.ds(1, nx - 1)])
    sent(S_GG, gg_recv.at[pl.ds(1, ntp - 1)])


def body(residual, attention, codes, absmax, down, up, gate, selected, counts, cotangent,
         nx=NX, nz=NZ, ny=NY):
    tokens, cols = residual.shape
    cap = attention.shape[0]
    heads, rank = down.shape
    slots = nz * cap
    hx = nx // NC
    ntp = ny * NC
    anywhere = pl.BlockSpec(memory_space=pl.ANY)
    vmem = pl.BlockSpec(memory_space=pltpu.VMEM)

    def f32(*shape):
        return pltpu.VMEM(shape, F32)

    def bf16(*shape):
        return pltpu.VMEM(shape, BF16)

    outs = pl.pallas_call(
        functools.partial(kernel, nx, nz, ny),
        out_shape=(
            jax.ShapeDtypeStruct((tokens, cols), BF16),
            jax.ShapeDtypeStruct((nx, nz, cap, heads), BF16),
            jax.ShapeDtypeStruct((rank, heads), F32),
            jax.ShapeDtypeStruct((rank, cols), F32),
            jax.ShapeDtypeStruct((1, cap), F32),
        ),
        in_specs=[anywhere] * 6 + [vmem, vmem, vmem, anywhere],
        out_specs=(anywhere, anywhere, anywhere, anywhere, vmem),
        scratch_shapes=[
            bf16(tokens, cols), pltpu.VMEM((heads, cols), jnp.int32), f32(*absmax.shape[::-1]),
            bf16(rank, cols), bf16(tokens, cols), f32(heads, cols),
            bf16(nx, slots, heads), bf16(nx, heads, cols), bf16(nx, rank, heads), bf16(slots, cols),
            f32(rank, slots), f32(rank, slots), f32(ny, rank // ny, slots), f32(ny, rank // ny, slots),
            f32(rank // ny, slots), f32(ny, rank // ny, slots),
            bf16(nx, nz, cap, heads), bf16(hx, nz, cap, heads), bf16(hx, nz, cap, heads),
            bf16(hx, ny, cap, heads), bf16(hx, cap, heads), bf16(hx, cap, heads),
            f32(nz, rank // nz, cols), f32(nz, rank // nz, cols), f32(rank // nz, cols),
            f32(nx, rank // nz, cols), f32(nz, rank // nz, cols),
            bf16(nz, cap, cols), bf16(nz, cap, cols), f32(cap, cols), bf16(tokens, cols),
            f32(nx, rank, heads), f32(nx, rank, heads), f32(rank, heads), f32(rank, cols),
            f32(8, 128), f32(ntp, 8, 128),
            pltpu.SemaphoreType.DMA((N_SEM,)), pltpu.SemaphoreType.DMA((N_SEM,)),
            pltpu.SemaphoreType.DMA((N_LOC,)),
        ],
        compiler_params=pltpu.CompilerParams(
            collective_id=0, has_side_effects=True, vmem_limit_bytes=56 << 20),
        name="block_step",
    )(residual, attention, codes, absmax.T, down.T, up, gate.reshape(1, cap), selected.reshape(1, cap),
      counts.reshape(1, 1), cotangent)
    new_res, head_grad, d_grad, u_grad, g_grad = outs
    return new_res, head_grad.reshape(nx * nz * cap, heads), d_grad.T, u_grad, g_grad.reshape(cap)


def solution(mesh):
    return jax.shard_map(
        body,
        mesh=mesh,
        in_specs=(
            P("seq", "tp"),
            P("seq", None),
            P("seq", "tp"),
            P("seq", "tp"),
            P("seq", None),
            P(None, "tp"),
            P("seq"),
            P("seq"),
            P("seq"),
            P("seq", "tp"),
        ),
        out_specs=(P("seq", "tp"), P(None, "seq"), P("seq", None), P(None, "tp"), P("seq")),
        check_vma=False,
    )
```

```python
import functools

import jax
import jax.numpy as jnp
from jax import lax
from jax.experimental import pallas as pl
from jax.experimental.pallas import tpu as pltpu
from jax.sharding import PartitionSpec as P

LEVELS = (
    -1.0,
    -0.6961928009986877,
    -0.5250730514526367,
    -0.39491748809814453,
    -0.28444138169288635,
    -0.18477343022823334,
    -0.09105003625154495,
    0.0,
    0.07958029955625534,
    0.16093020141124725,
    0.24611230194568634,
    0.33791524171829224,
    0.44070982933044434,
    0.5626170039176941,
    0.7229568362236023,
    1.0,
)
adapter_scale = 0.25
F32, BF16 = jnp.float32, jnp.bfloat16
MESH = pl.DeviceIdType.MESH

NX, NZ, NY, NC = 4, 8, 8, 2

(S_G, S_A, S_F, S_AZ, S_W1A, S_W1B, S_W3A, S_W3B, S_W2, S_DT, S_ASIB, S_RSIB, S_RRS, S_RAG,
 S_HSIB, S_HRS, S_FSIB, S_URS, S_UX, S_UAG, S_ORS, S_DX, S_GG, N_SEM) = (
    0, 1, 2, 4, *range(6, 16), 16, 18, 20, *range(22, 29))
(L_COT, L_CODES, L_ABS, L_DOWN, L_UP, L_RES, L_A, L_OUT, L_D, L_U, L_FOUT, N_LOC) = range(12)


def dot(a, b, ca, cb):
    return lax.dot_general(a, b, (((ca,), (cb,)), ((), ())), preferred_element_type=F32)


def split(value):
    high = value.astype(BF16)
    return high, (value - high.astype(F32)).astype(BF16)


def to_column(row, n):
    at = lax.broadcasted_iota(jnp.int32, (n, n), 0) == lax.broadcasted_iota(jnp.int32, (n, n), 1)
    return jnp.sum(jnp.where(at, jnp.broadcast_to(row, (n, n)), 0.0), axis=1, keepdims=True)


def to_row(column, n):
    at = lax.broadcasted_iota(jnp.int32, (n, n), 0) == lax.broadcasted_iota(jnp.int32, (n, n), 1)
    return jnp.sum(jnp.where(at, jnp.broadcast_to(column, (n, n)), 0.0), axis=0, keepdims=True)


def kernel(nx, nz, ny,
           res_hbm, attn, codes_hbm, abs_hbm, down_hbm, up_hbm, gate_ref, sel_ref, counts_ref, cot_hbm,
           out_res, out_ag, out_d, out_u, out_gate,
           res, codes, absm, up, cot, scales,
           a_all, w_all, dt_all, g_all,
           rt, rt_sib, rt_send, rt_recv, rag_send, rag,
           h_send, h_sib, hs, hr, f_send,
           u_send, u_recv, ux_send, ux_recv, uag,
           o_send, o_recv, o_home, new_res,
           d_send, d_recv, d_new, u_new, gg_send, gg_recv,
           ssem, rsem, lsem):
    tokens, cols = res.shape
    heads = w_all.shape[1]
    cap = gate_ref.shape[1]
    rank = up.shape[0]
    slots = nz * cap
    hx = nx // NC
    ntp = ny * NC

    seq = lax.axis_index("seq")
    tp = lax.axis_index("tp")
    x, z = seq // nz, seq % nz
    y, c = tp // NC, tp % NC

    def dev_x(k):
        return (((x + k) % nx) * nz + z, tp)

    def dev_z(k):
        return (x * nz + (z + k) % nz, tp)

    def dev_y(k):
        return (seq, ((y + k) % ny) * NC + c)

    def dev_tp(k):
        return (seq, (tp + k) % ntp)

    sibling = (seq, y * NC + (1 - c))

    def send(group, src, dst, device):
        pltpu.make_async_remote_copy(
            src_ref=src, dst_ref=dst, send_sem=ssem.at[group], recv_sem=rsem.at[group],
            device_id=device, device_id_type=MESH,
        ).start()

    def take(group, like):
        pltpu.make_async_copy(like, like, rsem.at[group]).wait()

    def sent(group, like):
        pltpu.make_async_copy(like, like, ssem.at[group]).wait()

    def local(which, src, dst):
        copy = pltpu.make_async_copy(src, dst, lsem.at[which])
        copy.start()
        return copy

    def gather(group, n, dev, parts):
        for k in (range(1, n) if n < 8 else (1, 7, 2, 6, 3, 5, 4)):
            for src, dst in zip(parts(0, 0), parts(0, k)):
                send(group, src, dst, dev(k))

    def g_parts(j, k):
        return [g_all.at[pl.ds(((j - k) % nz) * cap, cap)]]

    def g_like(n):
        return g_all.at[pl.ds(0, n * cap)]

    def a_part(j, n):
        row = ((y + j + n * (ny // 2)) % nz) * cap
        return a_all.at[hx * c + n, pl.ds(pl.multiple_of(row, cap), cap)]

    def a_parts(j, k):
        return [a_part(j, n) for n in range(hx)]

    def a_like(n):
        return a_all.at[pl.ds(hx * c, hx), pl.ds(0, n * cap)]

    def own(m):
        return jnp.where(c == 0, m, nx - 1 - m)

    def f_like(n):
        return out_ag.at[0, pl.ds(0, n)]

    def f_row(m):
        return (x + nx - own(m)) % nx

    cot_in = local(L_COT, cot_hbm, cot)
    codes_in = local(L_CODES, codes_hbm, codes)
    abs_in = local(L_ABS, abs_hbm, absm)
    down_in = local(L_DOWN, down_hbm, dt_all.at[0])
    up_in = local(L_UP, up_hbm, up)
    res_in = local(L_RES, res_hbm, res)

    barrier = pltpu.get_barrier_semaphore()
    for k in range(1, nx):
        pl.semaphore_signal(barrier, inc=1, device_id=dev_x(k), device_id_type=MESH)
    for k in range(1, nz):
        pl.semaphore_signal(barrier, inc=1, device_id=dev_z(k), device_id_type=MESH)
    for k in range(1, ntp):
        pl.semaphore_signal(barrier, inc=1, device_id=dev_tp(k), device_id_type=MESH)

    gate = to_column(gate_ref[...], cap)
    picked_token = to_column(sel_ref[...].astype(F32), cap)
    live = lax.broadcasted_iota(jnp.int32, (cap, tokens), 0) < counts_ref[...]
    pick = jnp.where(
        live & (lax.broadcasted_iota(jnp.int32, (cap, tokens), 1).astype(F32) == picked_token), 1.0, 0.0)
    pick_bf = pick.astype(BF16)
    cot_in.wait()
    upstream = dot(pick_bf, cot[...], 1, 0)
    g_all[pl.ds(0, cap), :] = (gate * upstream).astype(BF16)

    codes_in.wait()
    abs_in.wait()
    step = 32

    scale_high = absm[...].astype(BF16)
    rest = absm[...] - scale_high.astype(F32)
    scale_mid, scale_low = split(rest)
    qblocks = absm.shape[0]
    spread_to = jnp.where(
        lax.broadcasted_iota(jnp.int32, (qblocks, cols), 1) // (cols // qblocks)
        == lax.broadcasted_iota(jnp.int32, (qblocks, cols), 0), 1.0, 0.0).astype(BF16)
    scales[...] = (dot(scale_high, spread_to, 0, 0) + dot(scale_mid, spread_to, 0, 0)
                   + dot(scale_low, spread_to, 0, 0))

    def dequantize(n, carry):
        rows = pl.ds(pl.multiple_of(n * step, step), step)
        for q in range(cols // 128):
            code = codes[rows, pl.ds(q * 128, 128)]
            b0, b1, b2, b3 = [(code & (1 << bit)) != 0 for bit in range(4)]
            level = LEVELS
            for bit in (b0, b1, b2, b3):
                level = [jnp.where(bit, level[m + 1], level[m]) for m in range(0, len(level), 2)]
            scale = scales[rows, pl.ds(q * 128, 128)]
            w_all[0, rows, pl.ds(q * 128, 128)] = (level[0] * scale).astype(BF16)
        return carry

    lax.fori_loop(0, heads // step, dequantize, 0)
    down_in.wait()

    pl.semaphore_wait(barrier, (nx - 1) + (nz - 1) + (ntp - 1))

    for n in range(hx):
        off = (y + n * (ny // 2)) % nz
        i = hx * c + n
        dest = (z + nz - off) % nz
        at = pl.multiple_of((((x + i) % nx) * nz + dest) * heads, heads)
        block = attn.at[:, pl.ds(at, heads)]
        place = a_all.at[i, pl.ds(pl.multiple_of(off * cap, cap), cap)]

        @pl.when(off == 0)
        def _():
            local(L_A, block, place)

        @pl.when(off != 0)
        def _():
            send(S_AZ + n, block, place, (x * nz + dest, tp))

    gather(S_G, nz, dev_z, g_parts)
    hh = heads // 2
    first, second = pl.ds(0, hh), pl.ds(hh, hh)
    send(S_W3A, w_all.at[0, first], w_all.at[3, first], dev_x(1))
    send(S_W1A, w_all.at[0, second], w_all.at[1, second], dev_x(3))
    for k in range(1, nx):
        send(S_DT, dt_all.at[0], dt_all.at[nx - k], dev_x(k))
    send(S_W3B, w_all.at[0, second], w_all.at[3, second], dev_x(1))
    send(S_W1B, w_all.at[0, first], w_all.at[1, first], dev_x(3))

    for n in range(hx):
        off = (y + n * (ny // 2)) % nz

        @pl.when(off == 0)
        def _():
            place = a_all.at[0, pl.ds(0, cap)]
            pltpu.make_async_copy(place, place, lsem.at[L_A]).wait()

        @pl.when(off != 0)
        def _():
            take(S_AZ + n, a_all.at[0, pl.ds(0, cap)])
    gather(S_A, ny, dev_y, a_parts)
    half_w = w_all.at[0, first]
    take(S_W3A, half_w)
    send(S_W2, w_all.at[3, first], w_all.at[2, first], dev_x(1))
    take(S_W1A, half_w)
    send(S_W2, w_all.at[1, second], w_all.at[2, second], dev_x(3))

    up_in.wait()
    take(S_G, g_like(nz - 1))
    rank_part = (adapter_scale * dot(g_all[...], up[...], 1, 1)).astype(BF16)

    def head_block(i):
        part = dot(g_all[...], w_all[i], 1, 1) + dot(rank_part, dt_all[i], 1, 0)
        for j in range(nz):
            h_send[i, j] = part[j * cap:(j + 1) * cap].astype(BF16)

    def head_pair(m):
        send(S_HSIB + m, h_send.at[nx - 1 - own(m)], h_sib.at[m], sibling)

    def head_sum(m):
        take(S_HSIB + m, h_sib.at[m])
        for j in range(nz):
            hs[m, j] = (h_send[own(m), j].astype(F32) + h_sib[m, j].astype(F32)).astype(BF16)
        for k in range(1, ny):
            send(S_HRS + m, hs.at[m, (y + k) % ny], hr.at[m, ny - k], dev_y(k))

    def head_home(m):
        take(S_HRS + m, hr.at[m, pl.ds(1, ny - 1)])
        total = hs[m, y].astype(F32)
        for k in range(1, ny):
            total = total + hr[m, k].astype(F32)
        f_send[m] = total.astype(BF16)
        near = ((x + own(m)) % nx) * nz + z
        place = out_ag.at[x, shard_z]
        for k in (range(1, ny) if ny < 8 else (4, 3, 5, 2, 6, 1, 7)):
            send(S_F + m, f_send.at[m], place, (near, ((y + k) % ny) * NC + c))
        if m == 0:
            @pl.when(c == 0)
            def _():
                local(L_FOUT, f_send.at[0], place)

            @pl.when(c != 0)
            def _():
                send(S_F, f_send.at[0], place, (near, tp))
        else:
            send(S_F + m, f_send.at[m], place, (near, tp))

    def head_finish(m):
        if m == 0:
            @pl.when(c == 0)
            def _():
                take(S_F, f_like(ny - 1))
                pltpu.make_async_copy(f_send.at[0], f_send.at[0], lsem.at[L_FOUT]).wait()

            @pl.when(c != 0)
            def _():
                take(S_F, f_like(ny))
        else:
            take(S_F + m, f_like(ny))
        send(S_FSIB + m, out_ag.at[f_row(m)], out_ag.at[f_row(m)], sibling)

    shard_z = (z + y) % nz
    take(S_DT, dt_all.at[pl.ds(1, nx - 1)])
    head_block(0)
    take(S_W3B, half_w)
    head_block(3)
    head_pair(0)
    rt[...] = adapter_scale * dot(up[...], g_all[...], 1, 1)
    send(S_RSIB, rt, rt_sib, sibling)
    take(S_W1B, half_w)
    head_block(1)
    head_sum(0)
    take(S_W2, w_all.at[0])
    head_block(2)
    head_pair(1)
    take(S_A, a_like(ny - 1))
    a_mine = a_all.at[pl.ds(hx * c, hx)]
    send(S_ASIB, a_mine, a_mine, sibling)
    take(S_RSIB, rt_sib)
    for j in range(ny):
        rows = pl.ds(j * (rank // ny), rank // ny)
        rt_send[j] = rt[rows, :] + rt_sib[rows, :]
    for k in range(1, ny):
        send(S_RRS, rt_send.at[(y + k) % ny], rt_recv.at[ny - k], dev_y(k))
    head_sum(1)

    take(S_ASIB, a_mine)
    low = jnp.zeros((slots, rank), F32)
    low_t = jnp.zeros((rank, slots), F32)
    for i in range(nx):
        low = low + dot(a_all[i], dt_all[i], 1, 1)
        low_t = low_t + dot(dt_all[i], a_all[i], 1, 1)
    t_high, t_low = split(low_t)
    part = adapter_scale * (dot(t_high, g_all[...], 1, 0) + dot(t_low, g_all[...], 1, 0))
    for j in range(nz):
        u_send[j] = part[j * (rank // nz):(j + 1) * (rank // nz)]
    for k in range(1, nz):
        send(S_URS, u_send.at[(z + k) % nz], u_recv.at[nz - k], dev_z(k))

    high, small = split(adapter_scale * low)
    part = dot(high, up[...], 1, 0) + dot(small, up[...], 1, 0)
    for i in range(nx):
        part = part + dot(a_all[i], w_all[i], 1, 0)
    o_home[...] = part[:cap]
    for j in range(1, nz):
        o_send[j] = part[j * cap:(j + 1) * cap].astype(BF16)
    for k in range(1, nz):
        send(S_ORS, o_send.at[k], o_recv.at[nz - k], dev_z(k))

    take(S_RRS, rt_recv.at[pl.ds(1, ny - 1)])
    total = rt_send[y]
    for k in range(1, ny):
        total = total + rt_recv[k]
    rag_send[...] = total.astype(BF16).astype(F32)
    rag[y] = rag_send[...]
    for k in range(1, ny):
        send(S_RAG, rag_send, rag.at[y], dev_y(k))

    head_home(0)
    head_home(1)

    take(S_RAG, rag.at[pl.ds(0, ny - 1)])
    full_rt = jnp.reshape(rag[...], (rank, slots)).astype(BF16)
    for i in range(nx):
        d_send[i] = dot(full_rt, a_all[i], 1, 0)
    for k in range(1, nx):
        send(S_DX, d_send.at[k], d_recv.at[nx - k], dev_x(k))

    take(S_URS, u_recv.at[pl.ds(1, nz - 1)])
    total = u_send[z]
    for k in range(1, nz):
        total = total + u_recv[k]
    ux_send[...] = total
    for k in range(1, nx):
        send(S_UX, ux_send, ux_recv.at[nx - k], dev_x(k))

    head_finish(0)

    take(S_ORS, o_recv.at[pl.ds(1, nz - 1)])
    block = o_home[...]
    for k in range(1, nz):
        block = block + o_recv[k].astype(F32)
    res_in.wait()
    gate_part = to_row(jnp.sum(upstream * block, axis=1, keepdims=True), cap)
    gg_send[...] = jnp.zeros_like(gg_send)
    gg_send[:, pl.ds(0, cap)] = jnp.broadcast_to(gate_part, (8, cap))
    for k in range(1, ntp):
        send(S_GG, gg_send, gg_recv.at[ntp - k], dev_tp(k))
    picked = dot(pick_bf, res[...], 1, 0)
    updated = (picked + gate * block).astype(BF16)
    spread = dot(pick_bf, updated, 0, 0)
    taken = dot(pick_bf, jnp.ones((cap, 128), BF16), 0, 0)[:, :1] > 0.5
    new_res[...] = jnp.where(taken, spread, res[...].astype(F32)).astype(BF16)
    out_copy = local(L_OUT, new_res, out_res)

    take(S_UX, ux_recv.at[pl.ds(1, nx - 1)])
    total = ux_send[...]
    for k in range(1, nx):
        total = total + ux_recv[k]
    ux_send_sum = total
    sent(S_UX, ux_recv.at[pl.ds(1, nx - 1)])
    ux_send[...] = ux_send_sum
    uag[z] = ux_send_sum
    for k in range(1, nz):
        send(S_UAG, ux_send, uag.at[z], dev_z(k))

    take(S_DX, d_recv.at[pl.ds(1, nx - 1)])
    total = d_send[0]
    for k in range(1, nx):
        total = total + d_recv[k]
    d_new[...] = total
    d_copy = local(L_D, d_new, out_d)

    head_finish(1)

    take(S_GG, gg_recv.at[pl.ds(1, ntp - 1)])
    total = gg_send[...]
    for k in range(1, ntp):
        total = total + gg_recv[k]
    out_gate[...] = total[:1, :cap]

    take(S_UAG, uag.at[pl.ds(0, nz - 1)])
    u_new[...] = jnp.reshape(uag[...], (rank, cols))
    u_copy = local(L_U, u_new, out_u)
    for m in range(hx):
        take(S_FSIB + m, out_ag.at[0])

    out_copy.wait()
    d_copy.wait()
    u_copy.wait()
    for n in range(hx):
        @pl.when((y + n * (ny // 2)) % nz != 0)
        def _():
            sent(S_AZ + n, a_all.at[0, pl.ds(0, cap)])
    sent(S_G, g_like(nz - 1))
    sent(S_A, a_like(ny - 1))

    @pl.when(c == 0)
    def _():
        sent(S_F, f_like(ny - 1))

    @pl.when(c != 0)
    def _():
        sent(S_F, f_like(ny))
    sent(S_F + 1, f_like(ny))
    for group in (S_W1A, S_W1B, S_W3A, S_W3B):
        sent(group, half_w)
    sent(S_W2, w_all.at[0])
    sent(S_DT, dt_all.at[pl.ds(1, nx - 1)])
    sent(S_ASIB, a_mine)
    sent(S_RSIB, rt)
    sent(S_RRS, rt_recv.at[pl.ds(1, ny - 1)])
    sent(S_RAG, rag.at[pl.ds(0, ny - 1)])
    for m in range(hx):
        sent(S_HSIB + m, h_sib.at[m])
        sent(S_HRS + m, hr.at[m, pl.ds(1, ny - 1)])
        sent(S_FSIB + m, out_ag.at[0])

    sent(S_URS, u_recv.at[pl.ds(1, nz - 1)])
    sent(S_UAG, uag.at[pl.ds(0, nz - 1)])
    sent(S_ORS, o_recv.at[pl.ds(1, nz - 1)])
    sent(S_DX, d_recv.at[pl.ds(1, nx - 1)])
    sent(S_GG, gg_recv.at[pl.ds(1, ntp - 1)])


def hand_over(*refs):
    n = (len(refs) - 1) // 2
    sems = refs[-1]
    copies = []
    for src, dst in zip(refs[:n], refs[n:2 * n]):
        pieces = src.shape[0] if len(src.shape) == 4 else 1
        for piece in range(pieces):
            at = pl.ds(piece, 1) if pieces > 1 else slice(None)
            copies.append(pltpu.make_async_copy(src.at[at], dst.at[at], sems.at[len(copies)]))
    for copy in copies:
        copy.start()
    for copy in copies:
        copy.wait()


def body(residual, attention, codes, absmax, down, up, gate, selected, counts, cotangent,
         nx=NX, nz=NZ, ny=NY):
    tokens, cols = residual.shape
    cap = attention.shape[0]
    heads, rank = down.shape
    slots = nz * cap
    hx = nx // NC
    ntp = ny * NC
    anywhere = pl.BlockSpec(memory_space=pl.ANY)
    vmem = pl.BlockSpec(memory_space=pltpu.VMEM)

    def f32(*shape):
        return pltpu.VMEM(shape, F32)

    def bf16(*shape):
        return pltpu.VMEM(shape, BF16)

    outs = pl.pallas_call(
        functools.partial(kernel, nx, nz, ny),
        out_shape=(
            jax.ShapeDtypeStruct((tokens, cols), BF16),
            jax.ShapeDtypeStruct((nx, nz, cap, heads), BF16),
            jax.ShapeDtypeStruct((rank, heads), F32),
            jax.ShapeDtypeStruct((rank, cols), F32),
            jax.ShapeDtypeStruct((1, cap), F32),
        ),
        in_specs=[anywhere] * 6 + [vmem, vmem, vmem, anywhere],
        out_specs=(anywhere, anywhere, anywhere, anywhere, vmem),
        scratch_shapes=[
            bf16(tokens, cols), pltpu.VMEM((heads, cols), jnp.int32), f32(*absmax.shape[::-1]),
            bf16(rank, cols), bf16(tokens, cols), f32(heads, cols),
            bf16(nx, slots, heads), bf16(nx, heads, cols), bf16(nx, rank, heads), bf16(slots, cols),
            f32(rank, slots), f32(rank, slots), f32(ny, rank // ny, slots), f32(ny, rank // ny, slots),
            f32(rank // ny, slots), f32(ny, rank // ny, slots),
            bf16(nx, nz, cap, heads), bf16(hx, nz, cap, heads), bf16(hx, nz, cap, heads),
            bf16(hx, ny, cap, heads), bf16(hx, cap, heads),
            f32(nz, rank // nz, cols), f32(nz, rank // nz, cols), f32(rank // nz, cols),
            f32(nx, rank // nz, cols), f32(nz, rank // nz, cols),
            bf16(nz, cap, cols), bf16(nz, cap, cols), f32(cap, cols), bf16(tokens, cols),
            f32(nx, rank, heads), f32(nx, rank, heads), f32(rank, heads), f32(rank, cols),
            f32(8, 128), f32(ntp, 8, 128),
            pltpu.SemaphoreType.DMA((N_SEM,)), pltpu.SemaphoreType.DMA((N_SEM,)),
            pltpu.SemaphoreType.DMA((N_LOC,)),
        ],
        compiler_params=pltpu.CompilerParams(
            collective_id=0, has_side_effects=True, vmem_limit_bytes=56 << 20),
        name="block_step",
    )(residual, attention, codes, absmax.T, down.T, up, gate.reshape(1, cap), selected.reshape(1, cap),
      counts.reshape(1, 1), cotangent)
    new_res, head_grad, d_grad, u_grad, g_grad = pl.pallas_call(
        hand_over,
        out_shape=[jax.ShapeDtypeStruct(out.shape, out.dtype) for out in outs],
        in_specs=[anywhere] * 5,
        out_specs=[anywhere] * 5,
        scratch_shapes=[pltpu.SemaphoreType.DMA((nx + 4,))],
        name="hand_over",
    )(*outs)
    return new_res, head_grad.reshape(nx * nz * cap, heads), d_grad.T, u_grad, g_grad.reshape(cap)


def solution(mesh):
    return jax.shard_map(
        body,
        mesh=mesh,
        in_specs=(
            P("seq", "tp"),
            P("seq", None),
            P("seq", "tp"),
            P("seq", "tp"),
            P("seq", None),
            P(None, "tp"),
            P("seq"),
            P("seq"),
            P("seq"),
            P("seq", "tp"),
        ),
        out_specs=(P("seq", "tp"), P(None, "seq"), P("seq", None), P(None, "tp"), P("seq")),
        check_vma=False,
    )
```

```python
import functools

import jax
import jax.numpy as jnp
from jax import lax
from jax.experimental import pallas as pl
from jax.experimental.pallas import tpu as pltpu
from jax.sharding import PartitionSpec as P

LEVELS = (
    -1.0,
    -0.6961928009986877,
    -0.5250730514526367,
    -0.39491748809814453,
    -0.28444138169288635,
    -0.18477343022823334,
    -0.09105003625154495,
    0.0,
    0.07958029955625534,
    0.16093020141124725,
    0.24611230194568634,
    0.33791524171829224,
    0.44070982933044434,
    0.5626170039176941,
    0.7229568362236023,
    1.0,
)
adapter_scale = 0.25
F32, BF16 = jnp.float32, jnp.bfloat16
MESH = pl.DeviceIdType.MESH

NX, NZ, NY, NC = 4, 8, 8, 2

(S_G, S_A, S_F, S_AZ, S_W1A, S_W1B, S_W3A, S_W3B, S_W2, S_DT, S_ASIB, S_RSIB, S_RRS, S_RAG,
 S_HSIB, S_HRS, S_FSIB, S_URS, S_UX, S_UAG, S_ORS, S_DX, S_GG, N_SEM) = (
    0, 1, 2, 4, *range(6, 16), 16, 18, 20, *range(22, 29))
(L_COT, L_CODES, L_ABS, L_DOWN, L_UP, L_RES, L_A, L_OUT, L_D, L_U, L_FOUT, L_AG, N_LOC) = (*range(12), 15)


def dot(a, b, ca, cb):
    return lax.dot_general(a, b, (((ca,), (cb,)), ((), ())), preferred_element_type=F32)


def split(value):
    high = value.astype(BF16)
    return high, (value - high.astype(F32)).astype(BF16)


def to_column(row, n):
    at = lax.broadcasted_iota(jnp.int32, (n, n), 0) == lax.broadcasted_iota(jnp.int32, (n, n), 1)
    return jnp.sum(jnp.where(at, jnp.broadcast_to(row, (n, n)), 0.0), axis=1, keepdims=True)


def to_row(column, n):
    at = lax.broadcasted_iota(jnp.int32, (n, n), 0) == lax.broadcasted_iota(jnp.int32, (n, n), 1)
    return jnp.sum(jnp.where(at, jnp.broadcast_to(column, (n, n)), 0.0), axis=0, keepdims=True)


def kernel(nx, nz, ny,
           res_hbm, attn, codes_hbm, abs_hbm, down_hbm, up_hbm, gate_ref, sel_ref, counts_ref, cot_hbm,
           out_res, out_ag, out_d, out_u, out_gate,
           res, codes, absm, up, cot, scales,
           a_all, w_all, dt_all, g_all,
           rt, rt_sib, rt_send, rt_recv, rag_send, rag,
           h_send, h_sib, hs, hr, f_send, og,
           u_send, u_recv, ux_send, ux_recv, uag,
           o_send, o_recv, o_home, new_res,
           d_send, d_recv, d_new, u_new, gg_send, gg_recv,
           ssem, rsem, lsem):
    tokens, cols = res.shape
    heads = w_all.shape[1]
    cap = gate_ref.shape[1]
    rank = up.shape[0]
    slots = nz * cap
    hx = nx // NC
    ntp = ny * NC

    seq = lax.axis_index("seq")
    tp = lax.axis_index("tp")
    x, z = seq // nz, seq % nz
    y, c = tp // NC, tp % NC

    def dev_x(k):
        return (((x + k) % nx) * nz + z, tp)

    def dev_z(k):
        return (x * nz + (z + k) % nz, tp)

    def dev_y(k):
        return (seq, ((y + k) % ny) * NC + c)

    def dev_tp(k):
        return (seq, (tp + k) % ntp)

    sibling = (seq, y * NC + (1 - c))

    def send(group, src, dst, device):
        pltpu.make_async_remote_copy(
            src_ref=src, dst_ref=dst, send_sem=ssem.at[group], recv_sem=rsem.at[group],
            device_id=device, device_id_type=MESH,
        ).start()

    def take(group, like):
        pltpu.make_async_copy(like, like, rsem.at[group]).wait()

    def sent(group, like):
        pltpu.make_async_copy(like, like, ssem.at[group]).wait()

    def local(which, src, dst):
        copy = pltpu.make_async_copy(src, dst, lsem.at[which])
        copy.start()
        return copy

    def gather(group, n, dev, parts):
        for k in (range(1, n) if n < 8 else (1, 7, 2, 6, 3, 5, 4)):
            for src, dst in zip(parts(0, 0), parts(0, k)):
                send(group, src, dst, dev(k))

    def g_parts(j, k):
        return [g_all.at[pl.ds(((j - k) % nz) * cap, cap)]]

    def g_like(n):
        return g_all.at[pl.ds(0, n * cap)]

    def a_part(j, n):
        row = ((y + j + n * (ny // 2)) % nz) * cap
        return a_all.at[hx * c + n, pl.ds(pl.multiple_of(row, cap), cap)]

    def a_parts(j, k):
        return [a_part(j, n) for n in range(hx)]

    def a_like(n):
        return a_all.at[pl.ds(hx * c, hx), pl.ds(0, n * cap)]

    def own(m):
        return jnp.where(c == 0, m, nx - 1 - m)

    def f_like(n):
        return og.at[0, pl.ds(0, n)]

    def f_row(m):
        return (x + nx - own(m)) % nx

    cot_in = local(L_COT, cot_hbm, cot)
    codes_in = local(L_CODES, codes_hbm, codes)
    abs_in = local(L_ABS, abs_hbm, absm)
    down_in = local(L_DOWN, down_hbm, dt_all.at[0])
    up_in = local(L_UP, up_hbm, up)
    res_in = local(L_RES, res_hbm, res)

    barrier = pltpu.get_barrier_semaphore()
    for k in range(1, nx):
        pl.semaphore_signal(barrier, inc=1, device_id=dev_x(k), device_id_type=MESH)
    for k in range(1, nz):
        pl.semaphore_signal(barrier, inc=1, device_id=dev_z(k), device_id_type=MESH)
    for k in range(1, ntp):
        pl.semaphore_signal(barrier, inc=1, device_id=dev_tp(k), device_id_type=MESH)

    gate = to_column(gate_ref[...], cap)
    picked_token = to_column(sel_ref[...].astype(F32), cap)
    live = lax.broadcasted_iota(jnp.int32, (cap, tokens), 0) < counts_ref[...]
    pick = jnp.where(
        live & (lax.broadcasted_iota(jnp.int32, (cap, tokens), 1).astype(F32) == picked_token), 1.0, 0.0)
    pick_bf = pick.astype(BF16)
    cot_in.wait()
    upstream = dot(pick_bf, cot[...], 1, 0)
    g_all[pl.ds(0, cap), :] = (gate * upstream).astype(BF16)

    codes_in.wait()
    abs_in.wait()
    step = 32

    scale_high = absm[...].astype(BF16)
    rest = absm[...] - scale_high.astype(F32)
    scale_mid, scale_low = split(rest)
    qblocks = absm.shape[0]
    spread_to = jnp.where(
        lax.broadcasted_iota(jnp.int32, (qblocks, cols), 1) // (cols // qblocks)
        == lax.broadcasted_iota(jnp.int32, (qblocks, cols), 0), 1.0, 0.0).astype(BF16)
    scales[...] = (dot(scale_high, spread_to, 0, 0) + dot(scale_mid, spread_to, 0, 0)
                   + dot(scale_low, spread_to, 0, 0))

    def dequantize(n, carry):
        rows = pl.ds(pl.multiple_of(n * step, step), step)
        for q in range(cols // 128):
            code = codes[rows, pl.ds(q * 128, 128)]
            b0, b1, b2, b3 = [(code & (1 << bit)) != 0 for bit in range(4)]
            level = LEVELS
            for bit in (b0, b1, b2, b3):
                level = [jnp.where(bit, level[m + 1], level[m]) for m in range(0, len(level), 2)]
            scale = scales[rows, pl.ds(q * 128, 128)]
            w_all[0, rows, pl.ds(q * 128, 128)] = (level[0] * scale).astype(BF16)
        return carry

    lax.fori_loop(0, heads // step, dequantize, 0)
    down_in.wait()

    pl.semaphore_wait(barrier, (nx - 1) + (nz - 1) + (ntp - 1))

    for n in range(hx):
        off = (y + n * (ny // 2)) % nz
        i = hx * c + n
        dest = (z + nz - off) % nz
        at = pl.multiple_of((((x + i) % nx) * nz + dest) * heads, heads)
        block = attn.at[:, pl.ds(at, heads)]
        place = a_all.at[i, pl.ds(pl.multiple_of(off * cap, cap), cap)]

        @pl.when(off == 0)
        def _():
            local(L_A, block, place)

        @pl.when(off != 0)
        def _():
            send(S_AZ + n, block, place, (x * nz + dest, tp))

    gather(S_G, nz, dev_z, g_parts)
    hh = heads // 2
    first, second = pl.ds(0, hh), pl.ds(hh, hh)
    send(S_W3A, w_all.at[0, first], w_all.at[3, first], dev_x(1))
    send(S_W1A, w_all.at[0, second], w_all.at[1, second], dev_x(3))
    for k in range(1, nx):
        send(S_DT, dt_all.at[0], dt_all.at[nx - k], dev_x(k))
    send(S_W3B, w_all.at[0, second], w_all.at[3, second], dev_x(1))
    send(S_W1B, w_all.at[0, first], w_all.at[1, first], dev_x(3))

    for n in range(hx):
        off = (y + n * (ny // 2)) % nz

        @pl.when(off == 0)
        def _():
            place = a_all.at[0, pl.ds(0, cap)]
            pltpu.make_async_copy(place, place, lsem.at[L_A]).wait()

        @pl.when(off != 0)
        def _():
            take(S_AZ + n, a_all.at[0, pl.ds(0, cap)])
    gather(S_A, ny, dev_y, a_parts)
    half_w = w_all.at[0, first]
    take(S_W3A, half_w)
    send(S_W2, w_all.at[3, first], w_all.at[2, first], dev_x(1))
    take(S_W1A, half_w)
    send(S_W2, w_all.at[1, second], w_all.at[2, second], dev_x(3))

    up_in.wait()
    take(S_G, g_like(nz - 1))
    rank_part = (adapter_scale * dot(g_all[...], up[...], 1, 1)).astype(BF16)

    def head_block(i):
        part = dot(g_all[...], w_all[i], 1, 1) + dot(rank_part, dt_all[i], 1, 0)
        for j in range(nz):
            h_send[i, j] = part[j * cap:(j + 1) * cap].astype(BF16)

    def head_pair(m):
        send(S_HSIB + m, h_send.at[nx - 1 - own(m)], h_sib.at[m], sibling)

    def head_sum(m):
        take(S_HSIB + m, h_sib.at[m])
        for j in range(nz):
            hs[m, j] = (h_send[own(m), j].astype(F32) + h_sib[m, j].astype(F32)).astype(BF16)
        for k in range(1, ny):
            send(S_HRS + m, hs.at[m, (y + k) % ny], hr.at[m, ny - k], dev_y(k))

    def head_home(m):
        take(S_HRS + m, hr.at[m, pl.ds(1, ny - 1)])
        total = hs[m, y].astype(F32)
        for k in range(1, ny):
            total = total + hr[m, k].astype(F32)
        f_send[m] = total.astype(BF16)
        near = ((x + own(m)) % nx) * nz + z
        place = og.at[x, shard_z]
        for k in (range(1, ny) if ny < 8 else (4, 3, 5, 2, 6, 1, 7)):
            send(S_F + m, f_send.at[m], place, (near, ((y + k) % ny) * NC + c))
        if m == 0:
            @pl.when(c == 0)
            def _():
                local(L_FOUT, f_send.at[0], place)

            @pl.when(c != 0)
            def _():
                send(S_F, f_send.at[0], place, (near, tp))
        else:
            send(S_F + m, f_send.at[m], place, (near, tp))

    def head_finish(m):
        if m == 0:
            @pl.when(c == 0)
            def _():
                take(S_F, f_like(ny - 1))
                pltpu.make_async_copy(f_send.at[0], f_send.at[0], lsem.at[L_FOUT]).wait()

            @pl.when(c != 0)
            def _():
                take(S_F, f_like(ny))
        else:
            take(S_F + m, f_like(ny))
        send(S_FSIB + m, og.at[f_row(m)], og.at[f_row(m)], sibling)
        local(L_AG + m, og.at[f_row(m)], out_ag.at[f_row(m)])

    shard_z = (z + y) % nz
    take(S_DT, dt_all.at[pl.ds(1, nx - 1)])
    head_block(0)
    take(S_W3B, half_w)
    head_block(3)
    head_pair(0)
    rt[...] = adapter_scale * dot(up[...], g_all[...], 1, 1)
    send(S_RSIB, rt, rt_sib, sibling)
    take(S_W1B, half_w)
    head_block(1)
    head_sum(0)
    take(S_W2, w_all.at[0])
    head_block(2)
    head_pair(1)
    take(S_A, a_like(ny - 1))
    a_mine = a_all.at[pl.ds(hx * c, hx)]
    send(S_ASIB, a_mine, a_mine, sibling)
    take(S_RSIB, rt_sib)
    for j in range(ny):
        rows = pl.ds(j * (rank // ny), rank // ny)
        rt_send[j] = rt[rows, :] + rt_sib[rows, :]
    for k in range(1, ny):
        send(S_RRS, rt_send.at[(y + k) % ny], rt_recv.at[ny - k], dev_y(k))
    head_sum(1)

    take(S_ASIB, a_mine)
    low = jnp.zeros((slots, rank), F32)
    low_t = jnp.zeros((rank, slots), F32)
    for i in range(nx):
        low = low + dot(a_all[i], dt_all[i], 1, 1)
        low_t = low_t + dot(dt_all[i], a_all[i], 1, 1)
    t_high, t_low = split(low_t)
    part = adapter_scale * (dot(t_high, g_all[...], 1, 0) + dot(t_low, g_all[...], 1, 0))
    for j in range(nz):
        u_send[j] = part[j * (rank // nz):(j + 1) * (rank // nz)]
    for k in range(1, nz):
        send(S_URS, u_send.at[(z + k) % nz], u_recv.at[nz - k], dev_z(k))

    high, small = split(adapter_scale * low)
    part = dot(high, up[...], 1, 0) + dot(small, up[...], 1, 0)
    for i in range(nx):
        part = part + dot(a_all[i], w_all[i], 1, 0)
    o_home[...] = part[:cap]
    for j in range(1, nz):
        o_send[j] = part[j * cap:(j + 1) * cap].astype(BF16)
    for k in range(1, nz):
        send(S_ORS, o_send.at[k], o_recv.at[nz - k], dev_z(k))

    take(S_RRS, rt_recv.at[pl.ds(1, ny - 1)])
    total = rt_send[y]
    for k in range(1, ny):
        total = total + rt_recv[k]
    rag_send[...] = total.astype(BF16).astype(F32)
    rag[y] = rag_send[...]
    for k in range(1, ny):
        send(S_RAG, rag_send, rag.at[y], dev_y(k))

    head_home(0)
    head_home(1)

    take(S_RAG, rag.at[pl.ds(0, ny - 1)])
    full_rt = jnp.reshape(rag[...], (rank, slots)).astype(BF16)
    for i in range(nx):
        d_send[i] = dot(full_rt, a_all[i], 1, 0)
    for k in range(1, nx):
        send(S_DX, d_send.at[k], d_recv.at[nx - k], dev_x(k))

    take(S_URS, u_recv.at[pl.ds(1, nz - 1)])
    total = u_send[z]
    for k in range(1, nz):
        total = total + u_recv[k]
    ux_send[...] = total
    for k in range(1, nx):
        send(S_UX, ux_send, ux_recv.at[nx - k], dev_x(k))

    head_finish(0)

    take(S_ORS, o_recv.at[pl.ds(1, nz - 1)])
    block = o_home[...]
    for k in range(1, nz):
        block = block + o_recv[k].astype(F32)
    res_in.wait()
    gate_part = to_row(jnp.sum(upstream * block, axis=1, keepdims=True), cap)
    gg_send[...] = jnp.zeros_like(gg_send)
    gg_send[:, pl.ds(0, cap)] = jnp.broadcast_to(gate_part, (8, cap))
    for k in range(1, ntp):
        send(S_GG, gg_send, gg_recv.at[ntp - k], dev_tp(k))
    picked = dot(pick_bf, res[...], 1, 0)
    updated = (picked + gate * block).astype(BF16)
    spread = dot(pick_bf, updated, 0, 0)
    taken = dot(pick_bf, jnp.ones((cap, 128), BF16), 0, 0)[:, :1] > 0.5
    new_res[...] = jnp.where(taken, spread, res[...].astype(F32)).astype(BF16)
    out_copy = local(L_OUT, new_res, out_res)

    take(S_UX, ux_recv.at[pl.ds(1, nx - 1)])
    total = ux_send[...]
    for k in range(1, nx):
        total = total + ux_recv[k]
    ux_send_sum = total
    sent(S_UX, ux_recv.at[pl.ds(1, nx - 1)])
    ux_send[...] = ux_send_sum
    uag[z] = ux_send_sum
    for k in range(1, nz):
        send(S_UAG, ux_send, uag.at[z], dev_z(k))

    take(S_DX, d_recv.at[pl.ds(1, nx - 1)])
    total = d_send[0]
    for k in range(1, nx):
        total = total + d_recv[k]
    d_new[...] = total
    d_copy = local(L_D, d_new, out_d)

    head_finish(1)

    take(S_GG, gg_recv.at[pl.ds(1, ntp - 1)])
    total = gg_send[...]
    for k in range(1, ntp):
        total = total + gg_recv[k]
    out_gate[...] = total[:1, :cap]

    take(S_UAG, uag.at[pl.ds(0, nz - 1)])
    u_new[...] = jnp.reshape(uag[...], (rank, cols))
    u_copy = local(L_U, u_new, out_u)
    for m in range(hx):
        take(S_FSIB + m, og.at[0])
        row = (x + nx - (nx - 1 - own(m))) % nx
        local(L_AG + hx + m, og.at[row], out_ag.at[row])

    for m in range(2 * hx):
        pltpu.make_async_copy(og.at[0], og.at[0], lsem.at[L_AG + m]).wait()
    out_copy.wait()
    d_copy.wait()
    u_copy.wait()
    for n in range(hx):
        @pl.when((y + n * (ny // 2)) % nz != 0)
        def _():
            sent(S_AZ + n, a_all.at[0, pl.ds(0, cap)])
    sent(S_G, g_like(nz - 1))
    sent(S_A, a_like(ny - 1))

    @pl.when(c == 0)
    def _():
        sent(S_F, f_like(ny - 1))

    @pl.when(c != 0)
    def _():
        sent(S_F, f_like(ny))
    sent(S_F + 1, f_like(ny))
    for group in (S_W1A, S_W1B, S_W3A, S_W3B):
        sent(group, half_w)
    sent(S_W2, w_all.at[0])
    sent(S_DT, dt_all.at[pl.ds(1, nx - 1)])
    sent(S_ASIB, a_mine)
    sent(S_RSIB, rt)
    sent(S_RRS, rt_recv.at[pl.ds(1, ny - 1)])
    sent(S_RAG, rag.at[pl.ds(0, ny - 1)])
    for m in range(hx):
        sent(S_HSIB + m, h_sib.at[m])
        sent(S_HRS + m, hr.at[m, pl.ds(1, ny - 1)])
        sent(S_FSIB + m, og.at[0])

    sent(S_URS, u_recv.at[pl.ds(1, nz - 1)])
    sent(S_UAG, uag.at[pl.ds(0, nz - 1)])
    sent(S_ORS, o_recv.at[pl.ds(1, nz - 1)])
    sent(S_DX, d_recv.at[pl.ds(1, nx - 1)])
    sent(S_GG, gg_recv.at[pl.ds(1, ntp - 1)])


def hand_over(*refs):
    n = len(refs) // 3
    srcs, dsts, held, into, out_of = refs[:n], refs[n:2 * n], refs[2 * n:3 * n], refs[-2], refs[-1]
    ins, outs = [], []
    for src, dst, mid in zip(srcs, dsts, held):
        pieces = src.shape[0] if len(src.shape) == 4 else 1
        for piece in range(pieces):
            at = pl.ds(piece, 1) if pieces > 1 else slice(None)
            ins.append(pltpu.make_async_copy(src.at[at], mid.at[at], into.at[len(ins)]))
            outs.append(pltpu.make_async_copy(mid.at[at], dst.at[at], out_of.at[len(outs)]))
    for copy in ins:
        copy.start()
    for copy, onward in zip(ins, outs):
        copy.wait()
        onward.start()
    for copy in outs:
        copy.wait()


def body(residual, attention, codes, absmax, down, up, gate, selected, counts, cotangent,
         nx=NX, nz=NZ, ny=NY):
    tokens, cols = residual.shape
    cap = attention.shape[0]
    heads, rank = down.shape
    slots = nz * cap
    hx = nx // NC
    ntp = ny * NC
    anywhere = pl.BlockSpec(memory_space=pl.ANY)
    vmem = pl.BlockSpec(memory_space=pltpu.VMEM)

    def f32(*shape):
        return pltpu.VMEM(shape, F32)

    def bf16(*shape):
        return pltpu.VMEM(shape, BF16)

    outs = pl.pallas_call(
        functools.partial(kernel, nx, nz, ny),
        out_shape=(
            jax.ShapeDtypeStruct((tokens, cols), BF16),
            jax.ShapeDtypeStruct((nx, nz, cap, heads), BF16),
            jax.ShapeDtypeStruct((rank, heads), F32),
            jax.ShapeDtypeStruct((rank, cols), F32),
            jax.ShapeDtypeStruct((1, cap), F32),
        ),
        in_specs=[anywhere] * 6 + [vmem, vmem, vmem, anywhere],
        out_specs=(anywhere, anywhere, anywhere, anywhere, vmem),
        scratch_shapes=[
            bf16(tokens, cols), pltpu.VMEM((heads, cols), jnp.int32), f32(*absmax.shape[::-1]),
            bf16(rank, cols), bf16(tokens, cols), f32(heads, cols),
            bf16(nx, slots, heads), bf16(nx, heads, cols), bf16(nx, rank, heads), bf16(slots, cols),
            f32(rank, slots), f32(rank, slots), f32(ny, rank // ny, slots), f32(ny, rank // ny, slots),
            f32(rank // ny, slots), f32(ny, rank // ny, slots),
            bf16(nx, nz, cap, heads), bf16(hx, nz, cap, heads), bf16(hx, nz, cap, heads),
            bf16(hx, ny, cap, heads), bf16(hx, cap, heads), bf16(nx, nz, cap, heads),
            f32(nz, rank // nz, cols), f32(nz, rank // nz, cols), f32(rank // nz, cols),
            f32(nx, rank // nz, cols), f32(nz, rank // nz, cols),
            bf16(nz, cap, cols), bf16(nz, cap, cols), f32(cap, cols), bf16(tokens, cols),
            f32(nx, rank, heads), f32(nx, rank, heads), f32(rank, heads), f32(rank, cols),
            f32(8, 128), f32(ntp, 8, 128),
            pltpu.SemaphoreType.DMA((N_SEM,)), pltpu.SemaphoreType.DMA((N_SEM,)),
            pltpu.SemaphoreType.DMA((N_LOC,)),
        ],
        compiler_params=pltpu.CompilerParams(
            collective_id=0, has_side_effects=True, vmem_limit_bytes=56 << 20),
        name="block_step",
    )(residual, attention, codes, absmax.T, down.T, up, gate.reshape(1, cap), selected.reshape(1, cap),
      counts.reshape(1, 1), cotangent)
    new_res, head_grad, d_grad, u_grad, g_grad = pl.pallas_call(
        hand_over,
        out_shape=[jax.ShapeDtypeStruct(out.shape, out.dtype) for out in outs],
        in_specs=[anywhere] * 5,
        out_specs=[anywhere] * 5,
        scratch_shapes=[pltpu.VMEM(out.shape, out.dtype) for out in outs]
        + [pltpu.SemaphoreType.DMA((nx + 4,))] * 2,
        name="hand_over",
    )(*outs)
    return new_res, head_grad.reshape(nx * nz * cap, heads), d_grad.T, u_grad, g_grad.reshape(cap)


def solution(mesh):
    return jax.shard_map(
        body,
        mesh=mesh,
        in_specs=(
            P("seq", "tp"),
            P("seq", None),
            P("seq", "tp"),
            P("seq", "tp"),
            P("seq", None),
            P(None, "tp"),
            P("seq"),
            P("seq"),
            P("seq"),
            P("seq", "tp"),
        ),
        out_specs=(P("seq", "tp"), P(None, "seq"), P("seq", None), P(None, "tp"), P("seq")),
        check_vma=False,
    )
```

```python
import functools

import jax
import jax.numpy as jnp
from jax import lax
from jax.experimental import pallas as pl
from jax.experimental.pallas import tpu as pltpu
from jax.sharding import PartitionSpec as P

LEVELS = (
    -1.0,
    -0.6961928009986877,
    -0.5250730514526367,
    -0.39491748809814453,
    -0.28444138169288635,
    -0.18477343022823334,
    -0.09105003625154495,
    0.0,
    0.07958029955625534,
    0.16093020141124725,
    0.24611230194568634,
    0.33791524171829224,
    0.44070982933044434,
    0.5626170039176941,
    0.7229568362236023,
    1.0,
)
adapter_scale = 0.25
F32, BF16 = jnp.float32, jnp.bfloat16
MESH = pl.DeviceIdType.MESH

NX, NZ, NY, NC = 4, 8, 8, 2

(S_G, S_A, S_F0, S_F1, S_AZ, S_W1A, S_W1B, S_W3A, S_W3B, S_W2, S_DT, S_ASIB, S_RSIB, S_RRS, S_RAG,
 S_HSIB, S_HRS, S_FX, S_FSIB, S_URS, S_UX, S_UAG, S_ORS, S_DX, S_GG, N_SEM) = (
    0, 5, 10, 15, 20, *range(22, 32), 32, 34, 36, 38, *range(40, 47))
DIRECT = (S_A,)
(L_COT, L_CODES, L_ABS, L_DOWN, L_UP, L_RES, L_A, L_OUT, L_D, L_U, L_FOUT, L_AG, N_LOC) = (*range(11), 12, 16)


def dot(a, b, ca, cb):
    return lax.dot_general(a, b, (((ca,), (cb,)), ((), ())), preferred_element_type=F32)


def split(value):
    high = value.astype(BF16)
    return high, (value - high.astype(F32)).astype(BF16)


def to_column(row, n):
    at = lax.broadcasted_iota(jnp.int32, (n, n), 0) == lax.broadcasted_iota(jnp.int32, (n, n), 1)
    return jnp.sum(jnp.where(at, jnp.broadcast_to(row, (n, n)), 0.0), axis=1, keepdims=True)


def to_row(column, n):
    at = lax.broadcasted_iota(jnp.int32, (n, n), 0) == lax.broadcasted_iota(jnp.int32, (n, n), 1)
    return jnp.sum(jnp.where(at, jnp.broadcast_to(column, (n, n)), 0.0), axis=0, keepdims=True)


def kernel(nx, nz, ny,
           res_hbm, attn, codes_hbm, abs_hbm, down_hbm, up_hbm, gate_ref, sel_ref, counts_ref, cot_hbm,
           out_res, out_ag, out_d, out_u, out_gate,
           res, codes, absm, up, cot, scales,
           a_all, w_all, dt_all, g_all,
           rt, rt_sib, rt_send, rt_recv, rag_send, rag,
           h_send, h_sib, hs, hr, f_send, fx, og,
           u_send, u_recv, ux_send, ux_recv, uag,
           o_send, o_recv, o_home, new_res,
           d_send, d_recv, d_new, u_new, gg_send, gg_recv,
           ssem, rsem, lsem):
    tokens, cols = res.shape
    heads = w_all.shape[1]
    cap = gate_ref.shape[1]
    rank = up.shape[0]
    slots = nz * cap
    hx = nx // NC
    ntp = ny * NC

    seq = lax.axis_index("seq")
    tp = lax.axis_index("tp")
    x, z = seq // nz, seq % nz
    y, c = tp // NC, tp % NC

    def dev_x(k):
        return (((x + k) % nx) * nz + z, tp)

    def dev_z(k):
        return (x * nz + (z + k) % nz, tp)

    def dev_y(k):
        return (seq, ((y + k) % ny) * NC + c)

    def dev_tp(k):
        return (seq, (tp + k) % ntp)

    sibling = (seq, y * NC + (1 - c))

    def send(group, src, dst, device):
        pltpu.make_async_remote_copy(
            src_ref=src, dst_ref=dst, send_sem=ssem.at[group], recv_sem=rsem.at[group],
            device_id=device, device_id_type=MESH,
        ).start()

    def take(group, like):
        pltpu.make_async_copy(like, like, rsem.at[group]).wait()

    def sent(group, like):
        pltpu.make_async_copy(like, like, ssem.at[group]).wait()

    def local(which, src, dst):
        copy = pltpu.make_async_copy(src, dst, lsem.at[which])
        copy.start()
        return copy

    def gather_start(group, n, dev, parts):
        if n == 8 and group in DIRECT:
            for k in (1, 7, 2, 6, 3, 5, 4):
                for src, dst in zip(parts(0, 0), parts(0, k)):
                    send(group, src, dst, dev(k))
            return
        for k in sorted({1, n - 1} | ({2, n - 2} if n == 8 else set())):
            which = {n - 1: 0, 1: 1, n - 2: 2, 2: 3}[n - k] if n > 2 else 0
            for src, dst in zip(parts(0, 0), parts(0, k)):
                send(group + which, src, dst, dev(k))

    def gather_forward(group, n, dev, parts, halves, like):
        if n == 2 or (n == 8 and group in DIRECT):
            return
        far = n // 2 - 2
        for side, which in ((-1, 2 if far else 0), (1, 3 if far else 1)):
            j = side * (far if far else 1)
            take(group + which, like(1))
            if far:
                for src, dst in zip(parts(j, 0), parts(j, -side)):
                    send(group + 4, src, dst, dev(-side))
            half = 0 if side < 0 else 1
            k = -side * (n // 2 - abs(j))
            for src, dst in zip(halves(j, 0, half), halves(j, k, half)):
                send(group + 4, src, dst, dev(k))

    def gather_finish(group, n, like):
        if n == 8 and group in DIRECT:
            take(group, like(n - 1))
            return
        if n != 4:
            take(group, like(1))
        if n == 8:
            take(group + 1, like(1))
        if n > 2:
            take(group + 4, like(n // 2 - 1))

    def gather_sent(group, n, like):
        if n == 8 and group in DIRECT:
            sent(group, like(n - 1))
            return
        for which in range(4 if n == 8 else n // 2):
            sent(group + which, like(1))
        if n > 2:
            sent(group + 4, like(n // 2 - 1))

    def g_parts(j, k):
        return [g_all.at[pl.ds(((j - k) % nz) * cap, cap)]]

    def g_halves(j, k, half):
        return [g_all.at[pl.ds(((j - k) % nz) * cap, cap), pl.ds(half * (cols // 2), cols // 2)]]

    def g_like(n):
        return g_all.at[pl.ds(0, n * cap)]

    def a_part(j, n):
        row = ((y + j + n * (ny // 2)) % nz) * cap
        return a_all.at[hx * c + n, pl.ds(pl.multiple_of(row, cap), cap)]

    def a_parts(j, k):
        return [a_part(j, n) for n in range(hx)]

    def a_halves(j, k, half):
        return [a_part(j, half)]

    def a_like(n):
        return a_all.at[pl.ds(hx * c, hx), pl.ds(0, n * cap)]

    def own(m):
        return jnp.where(c == 0, m, nx - 1 - m)

    def f_row(m):
        return (x + nx - own(m)) % nx

    def f_parts(m):
        return lambda j, k: [fx.at[m] if (j, k) == (0, 0) else og.at[f_row(m), (z + y + j) % nz]]

    def f_halves(m):
        return lambda j, k, half: [
            og.at[f_row(m), (z + y + j) % nz, :, pl.ds(half * (heads // 2), heads // 2)]]

    def f_like(n):
        return og.at[0, pl.ds(0, n)]

    cot_in = local(L_COT, cot_hbm, cot)
    codes_in = local(L_CODES, codes_hbm, codes)
    abs_in = local(L_ABS, abs_hbm, absm)
    down_in = local(L_DOWN, down_hbm, dt_all.at[0])
    up_in = local(L_UP, up_hbm, up)
    res_in = local(L_RES, res_hbm, res)

    barrier = pltpu.get_barrier_semaphore()
    for k in range(1, nx):
        pl.semaphore_signal(barrier, inc=1, device_id=dev_x(k), device_id_type=MESH)
    for k in range(1, nz):
        pl.semaphore_signal(barrier, inc=1, device_id=dev_z(k), device_id_type=MESH)
    for k in range(1, ntp):
        pl.semaphore_signal(barrier, inc=1, device_id=dev_tp(k), device_id_type=MESH)

    gate = to_column(gate_ref[...], cap)
    picked_token = to_column(sel_ref[...].astype(F32), cap)
    live = lax.broadcasted_iota(jnp.int32, (cap, tokens), 0) < counts_ref[...]
    pick = jnp.where(
        live & (lax.broadcasted_iota(jnp.int32, (cap, tokens), 1).astype(F32) == picked_token), 1.0, 0.0)
    pick_bf = pick.astype(BF16)
    cot_in.wait()
    upstream = dot(pick_bf, cot[...], 1, 0)
    g_all[pl.ds(0, cap), :] = (gate * upstream).astype(BF16)

    codes_in.wait()
    abs_in.wait()
    step = 32

    scale_high = absm[...].astype(BF16)
    rest = absm[...] - scale_high.astype(F32)
    scale_mid, scale_low = split(rest)
    qblocks = absm.shape[0]
    spread_to = jnp.where(
        lax.broadcasted_iota(jnp.int32, (qblocks, cols), 1) // (cols // qblocks)
        == lax.broadcasted_iota(jnp.int32, (qblocks, cols), 0), 1.0, 0.0).astype(BF16)
    scales[...] = (dot(scale_high, spread_to, 0, 0) + dot(scale_mid, spread_to, 0, 0)
                   + dot(scale_low, spread_to, 0, 0))

    def dequantize(n, carry):
        rows = pl.ds(pl.multiple_of(n * step, step), step)
        for q in range(cols // 128):
            code = codes[rows, pl.ds(q * 128, 128)]
            b0, b1, b2, b3 = [(code & (1 << bit)) != 0 for bit in range(4)]
            level = LEVELS
            for bit in (b0, b1, b2, b3):
                level = [jnp.where(bit, level[m + 1], level[m]) for m in range(0, len(level), 2)]
            scale = scales[rows, pl.ds(q * 128, 128)]
            w_all[0, rows, pl.ds(q * 128, 128)] = (level[0] * scale).astype(BF16)
        return carry

    lax.fori_loop(0, heads // step, dequantize, 0)
    down_in.wait()

    pl.semaphore_wait(barrier, (nx - 1) + (nz - 1) + (ntp - 1))

    for n in range(hx):
        off = (y + n * (ny // 2)) % nz
        i = hx * c + n
        dest = (z + nz - off) % nz
        at = pl.multiple_of((((x + i) % nx) * nz + dest) * heads, heads)
        block = attn.at[:, pl.ds(at, heads)]
        place = a_all.at[i, pl.ds(pl.multiple_of(off * cap, cap), cap)]

        @pl.when(off == 0)
        def _():
            local(L_A, block, place)

        @pl.when(off != 0)
        def _():
            send(S_AZ + n, block, place, (x * nz + dest, tp))

    gather_start(S_G, nz, dev_z, g_parts)
    hh = heads // 2
    first, second = pl.ds(0, hh), pl.ds(hh, hh)
    send(S_W3A, w_all.at[0, first], w_all.at[3, first], dev_x(1))
    send(S_W1A, w_all.at[0, second], w_all.at[1, second], dev_x(3))
    for k in range(1, nx):
        send(S_DT, dt_all.at[0], dt_all.at[nx - k], dev_x(k))
    send(S_W3B, w_all.at[0, second], w_all.at[3, second], dev_x(1))
    send(S_W1B, w_all.at[0, first], w_all.at[1, first], dev_x(3))

    for n in range(hx):
        off = (y + n * (ny // 2)) % nz

        @pl.when(off == 0)
        def _():
            place = a_all.at[0, pl.ds(0, cap)]
            pltpu.make_async_copy(place, place, lsem.at[L_A]).wait()

        @pl.when(off != 0)
        def _():
            take(S_AZ + n, a_all.at[0, pl.ds(0, cap)])
    gather_start(S_A, ny, dev_y, a_parts)
    gather_forward(S_G, nz, dev_z, g_parts, g_halves, g_like)
    half_w = w_all.at[0, first]
    take(S_W3A, half_w)
    send(S_W2, w_all.at[3, first], w_all.at[2, first], dev_x(1))
    take(S_W1A, half_w)
    send(S_W2, w_all.at[1, second], w_all.at[2, second], dev_x(3))
    gather_forward(S_A, ny, dev_y, a_parts, a_halves, a_like)

    up_in.wait()
    gather_finish(S_G, nz, g_like)
    rank_part = (adapter_scale * dot(g_all[...], up[...], 1, 1)).astype(BF16)

    def head_block(i):
        part = dot(g_all[...], w_all[i], 1, 1) + dot(rank_part, dt_all[i], 1, 0)
        for j in range(nz):
            h_send[i, j] = part[j * cap:(j + 1) * cap].astype(BF16)

    def head_pair(m):
        send(S_HSIB + m, h_send.at[nx - 1 - own(m)], h_sib.at[m], sibling)

    def head_sum(m):
        take(S_HSIB + m, h_sib.at[m])
        for j in range(nz):
            hs[m, j] = (h_send[own(m), j].astype(F32) + h_sib[m, j].astype(F32)).astype(BF16)
        for k in range(1, ny):
            send(S_HRS + m, hs.at[m, (y + k) % ny], hr.at[m, ny - k], dev_y(k))

    def head_home(m):
        take(S_HRS + m, hr.at[m, pl.ds(1, ny - 1)])
        total = hs[m, y].astype(F32)
        for k in range(1, ny):
            total = total + hr[m, k].astype(F32)
        f_send[m] = total.astype(BF16)
        if m == 0:
            @pl.when(c == 0)
            def _():
                fx[0] = f_send[0]

            @pl.when(c != 0)
            def _():
                send(S_FX, f_send.at[0], fx.at[0], dev_x(nx - 1))
        else:
            send(S_FX + m, f_send.at[m], fx.at[m], dev_x(own(m)))

    def head_gather(m):
        if m == 0:
            @pl.when(c != 0)
            def _():
                take(S_FX, fx.at[0])
        else:
            take(S_FX + m, fx.at[m])
        local(L_FOUT + m, fx.at[m], og.at[f_row(m), shard_z])
        gather_start(S_F0 + 5 * m, ny, dev_y, f_parts(m))

    def head_forward(m):
        gather_forward(S_F0 + 5 * m, ny, dev_y, f_parts(m), f_halves(m), f_like)

    def head_finish(m):
        gather_finish(S_F0 + 5 * m, ny, f_like)
        pltpu.make_async_copy(fx.at[m], fx.at[m], lsem.at[L_FOUT + m]).wait()
        send(S_FSIB + m, og.at[f_row(m)], og.at[f_row(m)], sibling)
        local(L_AG + m, og.at[f_row(m)], out_ag.at[f_row(m)])

    shard_z = (z + y) % nz
    take(S_DT, dt_all.at[pl.ds(1, nx - 1)])
    head_block(0)
    take(S_W3B, half_w)
    head_block(3)
    head_pair(0)
    rt[...] = adapter_scale * dot(up[...], g_all[...], 1, 1)
    send(S_RSIB, rt, rt_sib, sibling)
    take(S_W1B, half_w)
    head_block(1)
    head_sum(0)
    take(S_W2, w_all.at[0])
    head_block(2)
    head_pair(1)
    gather_finish(S_A, ny, a_like)
    a_mine = a_all.at[pl.ds(hx * c, hx)]
    send(S_ASIB, a_mine, a_mine, sibling)
    take(S_RSIB, rt_sib)
    for j in range(ny):
        rows = pl.ds(j * (rank // ny), rank // ny)
        rt_send[j] = rt[rows, :] + rt_sib[rows, :]
    for k in range(1, ny):
        send(S_RRS, rt_send.at[(y + k) % ny], rt_recv.at[ny - k], dev_y(k))
    head_sum(1)

    take(S_ASIB, a_mine)
    low = jnp.zeros((slots, rank), F32)
    low_t = jnp.zeros((rank, slots), F32)
    for i in range(nx):
        low = low + dot(a_all[i], dt_all[i], 1, 1)
        low_t = low_t + dot(dt_all[i], a_all[i], 1, 1)
    t_high, t_low = split(low_t)
    part = adapter_scale * (dot(t_high, g_all[...], 1, 0) + dot(t_low, g_all[...], 1, 0))
    for j in range(nz):
        u_send[j] = part[j * (rank // nz):(j + 1) * (rank // nz)]
    for k in range(1, nz):
        send(S_URS, u_send.at[(z + k) % nz], u_recv.at[nz - k], dev_z(k))

    high, small = split(adapter_scale * low)
    part = dot(high, up[...], 1, 0) + dot(small, up[...], 1, 0)
    for i in range(nx):
        part = part + dot(a_all[i], w_all[i], 1, 0)
    o_home[...] = part[:cap]
    for j in range(1, nz):
        o_send[j] = part[j * cap:(j + 1) * cap].astype(BF16)
    for k in range(1, nz):
        send(S_ORS, o_send.at[k], o_recv.at[nz - k], dev_z(k))

    take(S_RRS, rt_recv.at[pl.ds(1, ny - 1)])
    total = rt_send[y]
    for k in range(1, ny):
        total = total + rt_recv[k]
    rag_send[...] = total.astype(BF16).astype(F32)
    rag[y] = rag_send[...]
    for k in range(1, ny):
        send(S_RAG, rag_send, rag.at[y], dev_y(k))

    head_home(0)
    head_home(1)
    head_gather(0)

    take(S_RAG, rag.at[pl.ds(0, ny - 1)])
    full_rt = jnp.reshape(rag[...], (rank, slots)).astype(BF16)
    for i in range(nx):
        d_send[i] = dot(full_rt, a_all[i], 1, 0)
    for k in range(1, nx):
        send(S_DX, d_send.at[k], d_recv.at[nx - k], dev_x(k))
    head_gather(1)
    head_forward(0)

    take(S_URS, u_recv.at[pl.ds(1, nz - 1)])
    total = u_send[z]
    for k in range(1, nz):
        total = total + u_recv[k]
    ux_send[...] = total
    for k in range(1, nx):
        send(S_UX, ux_send, ux_recv.at[nx - k], dev_x(k))

    head_forward(1)
    take(S_ORS, o_recv.at[pl.ds(1, nz - 1)])
    block = o_home[...]
    for k in range(1, nz):
        block = block + o_recv[k].astype(F32)
    res_in.wait()
    gate_part = to_row(jnp.sum(upstream * block, axis=1, keepdims=True), cap)
    gg_send[...] = jnp.zeros_like(gg_send)
    gg_send[:, pl.ds(0, cap)] = jnp.broadcast_to(gate_part, (8, cap))
    for k in range(1, ntp):
        send(S_GG, gg_send, gg_recv.at[ntp - k], dev_tp(k))
    picked = dot(pick_bf, res[...], 1, 0)
    updated = (picked + gate * block).astype(BF16)
    spread = dot(pick_bf, updated, 0, 0)
    taken = dot(pick_bf, jnp.ones((cap, 128), BF16), 0, 0)[:, :1] > 0.5
    new_res[...] = jnp.where(taken, spread, res[...].astype(F32)).astype(BF16)
    out_copy = local(L_OUT, new_res, out_res)

    take(S_UX, ux_recv.at[pl.ds(1, nx - 1)])
    total = ux_send[...]
    for k in range(1, nx):
        total = total + ux_recv[k]
    ux_send_sum = total
    sent(S_UX, ux_recv.at[pl.ds(1, nx - 1)])
    ux_send[...] = ux_send_sum
    uag[z] = ux_send_sum
    for k in range(1, nz):
        send(S_UAG, ux_send, uag.at[z], dev_z(k))

    take(S_DX, d_recv.at[pl.ds(1, nx - 1)])
    total = d_send[0]
    for k in range(1, nx):
        total = total + d_recv[k]
    d_new[...] = total
    d_copy = local(L_D, d_new, out_d)

    for m in range(hx):
        head_finish(m)

    take(S_GG, gg_recv.at[pl.ds(1, ntp - 1)])
    total = gg_send[...]
    for k in range(1, ntp):
        total = total + gg_recv[k]
    out_gate[...] = total[:1, :cap]

    take(S_UAG, uag.at[pl.ds(0, nz - 1)])
    u_new[...] = jnp.reshape(uag[...], (rank, cols))
    u_copy = local(L_U, u_new, out_u)
    for m in range(hx):
        take(S_FSIB + m, og.at[0])
        row = (x + nx - (nx - 1 - own(m))) % nx
        local(L_AG + hx + m, og.at[row], out_ag.at[row])

    for m in range(2 * hx):
        pltpu.make_async_copy(og.at[0], og.at[0], lsem.at[L_AG + m]).wait()
    out_copy.wait()
    d_copy.wait()
    u_copy.wait()
    for n in range(hx):
        @pl.when((y + n * (ny // 2)) % nz != 0)
        def _():
            sent(S_AZ + n, a_all.at[0, pl.ds(0, cap)])
    gather_sent(S_G, nz, g_like)
    gather_sent(S_A, ny, a_like)
    for m in range(hx):
        gather_sent(S_F0 + 5 * m, ny, f_like)
    for group in (S_W1A, S_W1B, S_W3A, S_W3B):
        sent(group, half_w)
    sent(S_W2, w_all.at[0])
    sent(S_DT, dt_all.at[pl.ds(1, nx - 1)])
    sent(S_ASIB, a_mine)
    sent(S_RSIB, rt)
    sent(S_RRS, rt_recv.at[pl.ds(1, ny - 1)])
    sent(S_RAG, rag.at[pl.ds(0, ny - 1)])
    for m in range(hx):
        sent(S_HSIB + m, h_sib.at[m])
        sent(S_HRS + m, hr.at[m, pl.ds(1, ny - 1)])
        sent(S_FSIB + m, og.at[0])

    @pl.when(c != 0)
    def _():
        sent(S_FX, fx.at[0])
    sent(S_FX + 1, fx.at[1])
    sent(S_URS, u_recv.at[pl.ds(1, nz - 1)])
    sent(S_UAG, uag.at[pl.ds(0, nz - 1)])
    sent(S_ORS, o_recv.at[pl.ds(1, nz - 1)])
    sent(S_DX, d_recv.at[pl.ds(1, nx - 1)])
    sent(S_GG, gg_recv.at[pl.ds(1, ntp - 1)])


def hand_over(*refs):
    n = len(refs) // 3
    srcs, dsts, held, into, out_of = refs[:n], refs[n:2 * n], refs[2 * n:3 * n], refs[-2], refs[-1]
    ins, outs = [], []
    for src, dst, mid in zip(srcs, dsts, held):
        pieces = src.shape[0] if len(src.shape) == 4 else 1
        for piece in range(pieces):
            at = pl.ds(piece, 1) if pieces > 1 else slice(None)
            ins.append(pltpu.make_async_copy(src.at[at], mid.at[at], into.at[len(ins)]))
            outs.append(pltpu.make_async_copy(mid.at[at], dst.at[at], out_of.at[len(outs)]))
    for copy in ins:
        copy.start()
    for copy, onward in zip(ins, outs):
        copy.wait()
        onward.start()
    for copy in outs:
        copy.wait()


def body(residual, attention, codes, absmax, down, up, gate, selected, counts, cotangent,
         nx=NX, nz=NZ, ny=NY):
    tokens, cols = residual.shape
    cap = attention.shape[0]
    heads, rank = down.shape
    slots = nz * cap
    hx = nx // NC
    ntp = ny * NC
    anywhere = pl.BlockSpec(memory_space=pl.ANY)
    vmem = pl.BlockSpec(memory_space=pltpu.VMEM)

    def f32(*shape):
        return pltpu.VMEM(shape, F32)

    def bf16(*shape):
        return pltpu.VMEM(shape, BF16)

    outs = pl.pallas_call(
        functools.partial(kernel, nx, nz, ny),
        out_shape=(
            jax.ShapeDtypeStruct((tokens, cols), BF16),
            jax.ShapeDtypeStruct((nx, nz, cap, heads), BF16),
            jax.ShapeDtypeStruct((rank, heads), F32),
            jax.ShapeDtypeStruct((rank, cols), F32),
            jax.ShapeDtypeStruct((1, cap), F32),
        ),
        in_specs=[anywhere] * 6 + [vmem, vmem, vmem, anywhere],
        out_specs=(anywhere, anywhere, anywhere, anywhere, vmem),
        scratch_shapes=[
            bf16(tokens, cols), pltpu.VMEM((heads, cols), jnp.int32), f32(*absmax.shape[::-1]),
            bf16(rank, cols), bf16(tokens, cols), f32(heads, cols),
            bf16(nx, slots, heads), bf16(nx, heads, cols), bf16(nx, rank, heads), bf16(slots, cols),
            f32(rank, slots), f32(rank, slots), f32(ny, rank // ny, slots), f32(ny, rank // ny, slots),
            f32(rank // ny, slots), f32(ny, rank // ny, slots),
            bf16(nx, nz, cap, heads), bf16(hx, nz, cap, heads), bf16(hx, nz, cap, heads),
            bf16(hx, ny, cap, heads), bf16(hx, cap, heads), bf16(hx, cap, heads), bf16(nx, nz, cap, heads),
            f32(nz, rank // nz, cols), f32(nz, rank // nz, cols), f32(rank // nz, cols),
            f32(nx, rank // nz, cols), f32(nz, rank // nz, cols),
            bf16(nz, cap, cols), bf16(nz, cap, cols), f32(cap, cols), bf16(tokens, cols),
            f32(nx, rank, heads), f32(nx, rank, heads), f32(rank, heads), f32(rank, cols),
            f32(8, 128), f32(ntp, 8, 128),
            pltpu.SemaphoreType.DMA((N_SEM,)), pltpu.SemaphoreType.DMA((N_SEM,)),
            pltpu.SemaphoreType.DMA((N_LOC,)),
        ],
        compiler_params=pltpu.CompilerParams(
            collective_id=0, has_side_effects=True, vmem_limit_bytes=56 << 20),
        name="block_step",
    )(residual, attention, codes, absmax.T, down.T, up, gate.reshape(1, cap), selected.reshape(1, cap),
      counts.reshape(1, 1), cotangent)
    new_res, head_grad, d_grad, u_grad, g_grad = pl.pallas_call(
        hand_over,
        out_shape=[jax.ShapeDtypeStruct(out.shape, out.dtype) for out in outs],
        in_specs=[anywhere] * 5,
        out_specs=[anywhere] * 5,
        scratch_shapes=[pltpu.VMEM(out.shape, out.dtype) for out in outs]
        + [pltpu.SemaphoreType.DMA((nx + 4,))] * 2,
        name="hand_over",
    )(*outs)
    return new_res, head_grad.reshape(nx * nz * cap, heads), d_grad.T, u_grad, g_grad.reshape(cap)


def solution(mesh):
    return jax.shard_map(
        body,
        mesh=mesh,
        in_specs=(
            P("seq", "tp"),
            P("seq", None),
            P("seq", "tp"),
            P("seq", "tp"),
            P("seq", None),
            P(None, "tp"),
            P("seq"),
            P("seq"),
            P("seq"),
            P("seq", "tp"),
        ),
        out_specs=(P("seq", "tp"), P(None, "seq"), P("seq", None), P(None, "tp"), P("seq")),
        check_vma=False,
    )
```

```python
import functools

import jax
import jax.numpy as jnp
from jax import lax
from jax.experimental import pallas as pl
from jax.experimental.pallas import tpu as pltpu
from jax.sharding import PartitionSpec as P

LEVELS = (
    -1.0,
    -0.6961928009986877,
    -0.5250730514526367,
    -0.39491748809814453,
    -0.28444138169288635,
    -0.18477343022823334,
    -0.09105003625154495,
    0.0,
    0.07958029955625534,
    0.16093020141124725,
    0.24611230194568634,
    0.33791524171829224,
    0.44070982933044434,
    0.5626170039176941,
    0.7229568362236023,
    1.0,
)
adapter_scale = 0.25
F32, BF16 = jnp.float32, jnp.bfloat16
MESH = pl.DeviceIdType.MESH

NX, NZ, NY, NC = 4, 8, 8, 2

(S_G, S_A, S_F0, S_F1, S_AZ, S_W1A, S_W1B, S_W3A, S_W3B, S_W2, S_DT, S_ASIB, S_RSIB, S_RRS, S_RAG,
 S_HSIB, S_HRS, S_FX, S_FSIB, S_URS, S_UX, S_UAG, S_ORS, S_DX, S_GG, N_SEM) = (
    0, 5, 10, 15, 20, *range(22, 32), 32, 34, 36, 38, *range(40, 47))
DIRECT = (S_A, S_F0, S_F1)
(L_COT, L_CODES, L_ABS, L_DOWN, L_UP, L_RES, L_A, L_OUT, L_D, L_U, L_FOUT, L_AG, N_LOC) = (*range(11), 12, 16)


def dot(a, b, ca, cb):
    return lax.dot_general(a, b, (((ca,), (cb,)), ((), ())), preferred_element_type=F32)


def split(value):
    high = value.astype(BF16)
    return high, (value - high.astype(F32)).astype(BF16)


def to_column(row, n):
    at = lax.broadcasted_iota(jnp.int32, (n, n), 0) == lax.broadcasted_iota(jnp.int32, (n, n), 1)
    return jnp.sum(jnp.where(at, jnp.broadcast_to(row, (n, n)), 0.0), axis=1, keepdims=True)


def to_row(column, n):
    at = lax.broadcasted_iota(jnp.int32, (n, n), 0) == lax.broadcasted_iota(jnp.int32, (n, n), 1)
    return jnp.sum(jnp.where(at, jnp.broadcast_to(column, (n, n)), 0.0), axis=0, keepdims=True)


def kernel(nx, nz, ny,
           res_hbm, attn, codes_hbm, abs_hbm, down_hbm, up_hbm, gate_ref, sel_ref, counts_ref, cot_hbm,
           out_res, out_ag, out_d, out_u, out_gate,
           res, codes, absm, up, cot, scales,
           a_all, w_all, dt_all, g_all,
           rt, rt_sib, rt_send, rt_recv, rag_send, rag,
           h_send, h_sib, hs, hr, fx, og,
           u_send, u_recv, ux_send, ux_recv, uag,
           o_send, o_recv, o_home, new_res,
           d_send, d_recv, d_new, u_new, gg_send, gg_recv,
           ssem, rsem, lsem):
    tokens, cols = res.shape
    heads = w_all.shape[1]
    cap = gate_ref.shape[1]
    rank = up.shape[0]
    slots = nz * cap
    hx = nx // NC
    ntp = ny * NC

    seq = lax.axis_index("seq")
    tp = lax.axis_index("tp")
    x, z = seq // nz, seq % nz
    y, c = tp // NC, tp % NC

    def dev_x(k):
        return (((x + k) % nx) * nz + z, tp)

    def dev_z(k):
        return (x * nz + (z + k) % nz, tp)

    def dev_y(k):
        return (seq, ((y + k) % ny) * NC + c)

    def dev_tp(k):
        return (seq, (tp + k) % ntp)

    sibling = (seq, y * NC + (1 - c))

    def send(group, src, dst, device):
        pltpu.make_async_remote_copy(
            src_ref=src, dst_ref=dst, send_sem=ssem.at[group], recv_sem=rsem.at[group],
            device_id=device, device_id_type=MESH,
        ).start()

    def take(group, like):
        pltpu.make_async_copy(like, like, rsem.at[group]).wait()

    def sent(group, like):
        pltpu.make_async_copy(like, like, ssem.at[group]).wait()

    def local(which, src, dst):
        copy = pltpu.make_async_copy(src, dst, lsem.at[which])
        copy.start()
        return copy

    def gather_start(group, n, dev, parts):
        if n == 8 and group in DIRECT:
            for k in (1, 7, 2, 6, 3, 5, 4):
                for src, dst in zip(parts(0, 0), parts(0, k)):
                    send(group, src, dst, dev(k))
            return
        for k in sorted({1, n - 1} | ({2, n - 2} if n == 8 else set())):
            which = {n - 1: 0, 1: 1, n - 2: 2, 2: 3}[n - k] if n > 2 else 0
            for src, dst in zip(parts(0, 0), parts(0, k)):
                send(group + which, src, dst, dev(k))

    def gather_forward(group, n, dev, parts, halves, like):
        if n == 2 or (n == 8 and group in DIRECT):
            return
        far = n // 2 - 2
        for side, which in ((-1, 2 if far else 0), (1, 3 if far else 1)):
            j = side * (far if far else 1)
            take(group + which, like(1))
            if far:
                for src, dst in zip(parts(j, 0), parts(j, -side)):
                    send(group + 4, src, dst, dev(-side))
            half = 0 if side < 0 else 1
            k = -side * (n // 2 - abs(j))
            for src, dst in zip(halves(j, 0, half), halves(j, k, half)):
                send(group + 4, src, dst, dev(k))

    def gather_finish(group, n, like):
        if n == 8 and group in DIRECT:
            take(group, like(n - 1))
            return
        if n != 4:
            take(group, like(1))
        if n == 8:
            take(group + 1, like(1))
        if n > 2:
            take(group + 4, like(n // 2 - 1))

    def gather_sent(group, n, like):
        if n == 8 and group in DIRECT:
            sent(group, like(n - 1))
            return
        for which in range(4 if n == 8 else n // 2):
            sent(group + which, like(1))
        if n > 2:
            sent(group + 4, like(n // 2 - 1))

    def g_parts(j, k):
        return [g_all.at[pl.ds(((j - k) % nz) * cap, cap)]]

    def g_halves(j, k, half):
        return [g_all.at[pl.ds(((j - k) % nz) * cap, cap), pl.ds(half * (cols // 2), cols // 2)]]

    def g_like(n):
        return g_all.at[pl.ds(0, n * cap)]

    def a_part(j, n):
        row = ((y + j + n * (ny // 2)) % nz) * cap
        return a_all.at[hx * c + n, pl.ds(pl.multiple_of(row, cap), cap)]

    def a_parts(j, k):
        return [a_part(j, n) for n in range(hx)]

    def a_halves(j, k, half):
        return [a_part(j, half)]

    def a_like(n):
        return a_all.at[pl.ds(hx * c, hx), pl.ds(0, n * cap)]

    def own(m):
        return jnp.where(c == 0, m, nx - 1 - m)

    def f_row(m):
        return (x + nx - own(m)) % nx

    def f_parts(m):
        return lambda j, k: [fx.at[m] if (j, k) == (0, 0) else og.at[f_row(m), (z + y + j) % nz]]

    def f_halves(m):
        return lambda j, k, half: [
            og.at[f_row(m), (z + y + j) % nz, :, pl.ds(half * (heads // 2), heads // 2)]]

    def f_like(n):
        return og.at[0, pl.ds(0, n)]

    cot_in = local(L_COT, cot_hbm, cot)
    codes_in = local(L_CODES, codes_hbm, codes)
    abs_in = local(L_ABS, abs_hbm, absm)
    down_in = local(L_DOWN, down_hbm, dt_all.at[0])
    up_in = local(L_UP, up_hbm, up)
    res_in = local(L_RES, res_hbm, res)

    barrier = pltpu.get_barrier_semaphore()
    for k in range(1, nx):
        pl.semaphore_signal(barrier, inc=1, device_id=dev_x(k), device_id_type=MESH)
    for k in range(1, nz):
        pl.semaphore_signal(barrier, inc=1, device_id=dev_z(k), device_id_type=MESH)
    for k in range(1, ntp):
        pl.semaphore_signal(barrier, inc=1, device_id=dev_tp(k), device_id_type=MESH)

    gate = to_column(gate_ref[...], cap)
    picked_token = to_column(sel_ref[...].astype(F32), cap)
    live = lax.broadcasted_iota(jnp.int32, (cap, tokens), 0) < counts_ref[...]
    pick = jnp.where(
        live & (lax.broadcasted_iota(jnp.int32, (cap, tokens), 1).astype(F32) == picked_token), 1.0, 0.0)
    pick_bf = pick.astype(BF16)
    cot_in.wait()
    upstream = dot(pick_bf, cot[...], 1, 0)
    g_all[pl.ds(0, cap), :] = (gate * upstream).astype(BF16)

    codes_in.wait()
    abs_in.wait()
    step = 32

    scale_high = absm[...].astype(BF16)
    rest = absm[...] - scale_high.astype(F32)
    scale_mid, scale_low = split(rest)
    qblocks = absm.shape[0]
    spread_to = jnp.where(
        lax.broadcasted_iota(jnp.int32, (qblocks, cols), 1) // (cols // qblocks)
        == lax.broadcasted_iota(jnp.int32, (qblocks, cols), 0), 1.0, 0.0).astype(BF16)
    scales[...] = (dot(scale_high, spread_to, 0, 0) + dot(scale_mid, spread_to, 0, 0)
                   + dot(scale_low, spread_to, 0, 0))

    def dequantize(n, carry):
        rows = pl.ds(pl.multiple_of(n * step, step), step)
        for q in range(cols // 128):
            code = codes[rows, pl.ds(q * 128, 128)]
            b0, b1, b2, b3 = [(code & (1 << bit)) != 0 for bit in range(4)]
            level = LEVELS
            for bit in (b0, b1, b2, b3):
                level = [jnp.where(bit, level[m + 1], level[m]) for m in range(0, len(level), 2)]
            scale = scales[rows, pl.ds(q * 128, 128)]
            w_all[0, rows, pl.ds(q * 128, 128)] = (level[0] * scale).astype(BF16)
        return carry

    lax.fori_loop(0, heads // step, dequantize, 0)
    down_in.wait()

    pl.semaphore_wait(barrier, (nx - 1) + (nz - 1) + (ntp - 1))

    for n in range(hx):
        off = (y + n * (ny // 2)) % nz
        i = hx * c + n
        dest = (z + nz - off) % nz
        at = pl.multiple_of((((x + i) % nx) * nz + dest) * heads, heads)
        block = attn.at[:, pl.ds(at, heads)]
        place = a_all.at[i, pl.ds(pl.multiple_of(off * cap, cap), cap)]

        @pl.when(off == 0)
        def _():
            local(L_A, block, place)

        @pl.when(off != 0)
        def _():
            send(S_AZ + n, block, place, (x * nz + dest, tp))

    gather_start(S_G, nz, dev_z, g_parts)
    hh = heads // 2
    first, second = pl.ds(0, hh), pl.ds(hh, hh)
    send(S_W3A, w_all.at[0, first], w_all.at[3, first], dev_x(1))
    send(S_W1A, w_all.at[0, second], w_all.at[1, second], dev_x(3))
    for k in range(1, nx):
        send(S_DT, dt_all.at[0], dt_all.at[nx - k], dev_x(k))
    send(S_W3B, w_all.at[0, second], w_all.at[3, second], dev_x(1))
    send(S_W1B, w_all.at[0, first], w_all.at[1, first], dev_x(3))

    for n in range(hx):
        off = (y + n * (ny // 2)) % nz

        @pl.when(off == 0)
        def _():
            place = a_all.at[0, pl.ds(0, cap)]
            pltpu.make_async_copy(place, place, lsem.at[L_A]).wait()

        @pl.when(off != 0)
        def _():
            take(S_AZ + n, a_all.at[0, pl.ds(0, cap)])
    gather_start(S_A, ny, dev_y, a_parts)
    gather_forward(S_G, nz, dev_z, g_parts, g_halves, g_like)
    half_w = w_all.at[0, first]
    take(S_W3A, half_w)
    send(S_W2, w_all.at[3, first], w_all.at[2, first], dev_x(1))
    take(S_W1A, half_w)
    send(S_W2, w_all.at[1, second], w_all.at[2, second], dev_x(3))
    gather_forward(S_A, ny, dev_y, a_parts, a_halves, a_like)

    up_in.wait()
    gather_finish(S_G, nz, g_like)
    rt[...] = adapter_scale * dot(up[...], g_all[...], 1, 1)
    send(S_RSIB, rt, rt_sib, sibling)
    rank_part = (adapter_scale * dot(g_all[...], up[...], 1, 1)).astype(BF16)

    def head_block(i):
        part = dot(g_all[...], w_all[i], 1, 1) + dot(rank_part, dt_all[i], 1, 0)
        for j in range(nz):
            h_send[i, j] = part[j * cap:(j + 1) * cap].astype(BF16)

    def head_pair(m):
        send(S_HSIB + m, h_send.at[nx - 1 - own(m)], h_sib.at[m], sibling)

    def head_sum(m):
        take(S_HSIB + m, h_sib.at[m])
        for j in range(nz):
            hs[m, j] = (h_send[own(m), j].astype(F32) + h_sib[m, j].astype(F32)).astype(BF16)
        near = ((x + own(m)) % nx) * nz + z
        for k in (4, 3, 5, 2, 6, 1, 7) if ny == 8 else range(1, ny):
            send(S_HRS + m, hs.at[m, (y + k) % ny], hr.at[m, ny - k], (near, ((y + k) % ny) * NC + c))
        if m == 0:
            @pl.when(c == 0)
            def _():
                hr[0, 0] = hs[0, y]

            @pl.when(c != 0)
            def _():
                send(S_HRS, hs.at[0, y], hr.at[0, 0], (near, tp))
        else:
            send(S_HRS + m, hs.at[m, y], hr.at[m, 0], (near, tp))

    def head_home(m):
        if m == 0:
            @pl.when(c == 0)
            def _():
                take(S_HRS, hr.at[0, pl.ds(1, ny - 1)])

            @pl.when(c != 0)
            def _():
                take(S_HRS, hr.at[0])
        else:
            take(S_HRS + m, hr.at[m])
        total = hr[m, 0].astype(F32)
        for k in range(1, ny):
            total = total + hr[m, k].astype(F32)
        fx[m] = total.astype(BF16)
        local(L_FOUT + m, fx.at[m], og.at[f_row(m), shard_z])
        gather_start(S_F0 + 5 * m, ny, dev_y, f_parts(m))

    def head_forward(m):
        gather_forward(S_F0 + 5 * m, ny, dev_y, f_parts(m), f_halves(m), f_like)

    def head_finish(m):
        gather_finish(S_F0 + 5 * m, ny, f_like)
        pltpu.make_async_copy(fx.at[m], fx.at[m], lsem.at[L_FOUT + m]).wait()
        send(S_FSIB + m, og.at[f_row(m)], og.at[f_row(m)], sibling)
        local(L_AG + m, og.at[f_row(m)], out_ag.at[f_row(m)])

    shard_z = (z + y) % nz
    take(S_DT, dt_all.at[pl.ds(1, nx - 1)])
    head_block(0)
    take(S_W3B, half_w)
    head_block(3)
    head_pair(0)
    take(S_RSIB, rt_sib)
    for j in range(ny):
        rows = pl.ds(j * (rank // ny), rank // ny)
        rt_send[j] = rt[rows, :] + rt_sib[rows, :]
    for k in range(1, ny):
        send(S_RRS, rt_send.at[(y + k) % ny], rt_recv.at[ny - k], dev_y(k))
    take(S_W1B, half_w)
    head_block(1)
    head_sum(0)
    take(S_W2, w_all.at[0])
    head_block(2)
    head_pair(1)
    gather_finish(S_A, ny, a_like)
    a_mine = a_all.at[pl.ds(hx * c, hx)]
    send(S_ASIB, a_mine, a_mine, sibling)
    head_sum(1)
    take(S_RRS, rt_recv.at[pl.ds(1, ny - 1)])
    total = rt_send[y]
    for k in range(1, ny):
        total = total + rt_recv[k]
    rag_send[...] = total.astype(BF16).astype(F32)
    rag[y] = rag_send[...]
    for k in range(1, ny):
        send(S_RAG, rag_send, rag.at[y], dev_y(k))


    take(S_ASIB, a_mine)
    low = jnp.zeros((slots, rank), F32)
    low_t = jnp.zeros((rank, slots), F32)
    for i in range(nx):
        low = low + dot(a_all[i], dt_all[i], 1, 1)
        low_t = low_t + dot(dt_all[i], a_all[i], 1, 1)
    t_high, t_low = split(low_t)
    part = adapter_scale * (dot(t_high, g_all[...], 1, 0) + dot(t_low, g_all[...], 1, 0))
    for j in range(nz):
        u_send[j] = part[j * (rank // nz):(j + 1) * (rank // nz)]
    for k in range(1, nz):
        send(S_URS, u_send.at[(z + k) % nz], u_recv.at[nz - k], dev_z(k))

    high, small = split(adapter_scale * low)
    part = dot(high, up[...], 1, 0) + dot(small, up[...], 1, 0)
    for i in range(nx):
        part = part + dot(a_all[i], w_all[i], 1, 0)
    o_home[...] = part[:cap]
    for j in range(1, nz):
        o_send[j] = part[j * cap:(j + 1) * cap].astype(BF16)
    for k in range(1, nz):
        send(S_ORS, o_send.at[k], o_recv.at[nz - k], dev_z(k))

    head_home(0)
    take(S_URS, u_recv.at[pl.ds(1, nz - 1)])
    total = u_send[z]
    for k in range(1, nz):
        total = total + u_recv[k]
    ux_send[...] = total
    for k in range(1, nx):
        send(S_UX, ux_send, ux_recv.at[nx - k], dev_x(k))

    head_home(1)

    take(S_RAG, rag.at[pl.ds(0, ny - 1)])
    full_rt = jnp.reshape(rag[...], (rank, slots)).astype(BF16)
    for i in range(nx):
        d_send[i] = dot(full_rt, a_all[i], 1, 0)
    for k in range(1, nx):
        send(S_DX, d_send.at[k], d_recv.at[nx - k], dev_x(k))
    head_forward(0)

    head_forward(1)
    take(S_ORS, o_recv.at[pl.ds(1, nz - 1)])
    block = o_home[...]
    for k in range(1, nz):
        block = block + o_recv[k].astype(F32)
    res_in.wait()
    gate_part = to_row(jnp.sum(upstream * block, axis=1, keepdims=True), cap)
    gg_send[...] = jnp.zeros_like(gg_send)
    gg_send[:, pl.ds(0, cap)] = jnp.broadcast_to(gate_part, (8, cap))
    for k in range(1, ntp):
        send(S_GG, gg_send, gg_recv.at[ntp - k], dev_tp(k))
    picked = dot(pick_bf, res[...], 1, 0)
    updated = (picked + gate * block).astype(BF16)
    spread = dot(pick_bf, updated, 0, 0)
    taken = dot(pick_bf, jnp.ones((cap, 128), BF16), 0, 0)[:, :1] > 0.5
    new_res[...] = jnp.where(taken, spread, res[...].astype(F32)).astype(BF16)
    out_copy = local(L_OUT, new_res, out_res)

    take(S_UX, ux_recv.at[pl.ds(1, nx - 1)])
    total = ux_send[...]
    for k in range(1, nx):
        total = total + ux_recv[k]
    ux_send_sum = total
    sent(S_UX, ux_recv.at[pl.ds(1, nx - 1)])
    ux_send[...] = ux_send_sum
    uag[z] = ux_send_sum
    for k in range(1, nz):
        send(S_UAG, ux_send, uag.at[z], dev_z(k))

    take(S_DX, d_recv.at[pl.ds(1, nx - 1)])
    total = d_send[0]
    for k in range(1, nx):
        total = total + d_recv[k]
    d_new[...] = total
    d_copy = local(L_D, d_new, out_d)

    for m in range(hx):
        head_finish(m)

    take(S_GG, gg_recv.at[pl.ds(1, ntp - 1)])
    total = gg_send[...]
    for k in range(1, ntp):
        total = total + gg_recv[k]
    out_gate[...] = total[:1, :cap]

    take(S_UAG, uag.at[pl.ds(0, nz - 1)])
    u_new[...] = jnp.reshape(uag[...], (rank, cols))
    u_copy = local(L_U, u_new, out_u)
    for m in range(hx):
        take(S_FSIB + m, og.at[0])
        row = (x + nx - (nx - 1 - own(m))) % nx
        local(L_AG + hx + m, og.at[row], out_ag.at[row])

    for m in range(2 * hx):
        pltpu.make_async_copy(og.at[0], og.at[0], lsem.at[L_AG + m]).wait()
    out_copy.wait()
    d_copy.wait()
    u_copy.wait()
    for n in range(hx):
        @pl.when((y + n * (ny // 2)) % nz != 0)
        def _():
            sent(S_AZ + n, a_all.at[0, pl.ds(0, cap)])
    gather_sent(S_G, nz, g_like)
    gather_sent(S_A, ny, a_like)
    for m in range(hx):
        gather_sent(S_F0 + 5 * m, ny, f_like)
    for group in (S_W1A, S_W1B, S_W3A, S_W3B):
        sent(group, half_w)
    sent(S_W2, w_all.at[0])
    sent(S_DT, dt_all.at[pl.ds(1, nx - 1)])
    sent(S_ASIB, a_mine)
    sent(S_RSIB, rt)
    sent(S_RRS, rt_recv.at[pl.ds(1, ny - 1)])
    sent(S_RAG, rag.at[pl.ds(0, ny - 1)])
    for m in range(hx):
        sent(S_HSIB + m, h_sib.at[m])
        sent(S_FSIB + m, og.at[0])

    @pl.when(c == 0)
    def _():
        sent(S_HRS, hr.at[0, pl.ds(1, ny - 1)])

    @pl.when(c != 0)
    def _():
        sent(S_HRS, hr.at[0])
    sent(S_HRS + 1, hr.at[1])
    sent(S_URS, u_recv.at[pl.ds(1, nz - 1)])
    sent(S_UAG, uag.at[pl.ds(0, nz - 1)])
    sent(S_ORS, o_recv.at[pl.ds(1, nz - 1)])
    sent(S_DX, d_recv.at[pl.ds(1, nx - 1)])
    sent(S_GG, gg_recv.at[pl.ds(1, ntp - 1)])


def hand_over(*refs):
    n = len(refs) // 3
    srcs, dsts, held, into, out_of = refs[:n], refs[n:2 * n], refs[2 * n:3 * n], refs[-2], refs[-1]
    ins, outs = [], []
    for src, dst, mid in zip(srcs, dsts, held):
        pieces = src.shape[0] if len(src.shape) == 4 else 1
        for piece in range(pieces):
            at = pl.ds(piece, 1) if pieces > 1 else slice(None)
            ins.append(pltpu.make_async_copy(src.at[at], mid.at[at], into.at[len(ins)]))
            outs.append(pltpu.make_async_copy(mid.at[at], dst.at[at], out_of.at[len(outs)]))
    for copy in ins:
        copy.start()
    for copy, onward in zip(ins, outs):
        copy.wait()
        onward.start()
    for copy in outs:
        copy.wait()


def body(residual, attention, codes, absmax, down, up, gate, selected, counts, cotangent,
         nx=NX, nz=NZ, ny=NY):
    tokens, cols = residual.shape
    cap = attention.shape[0]
    heads, rank = down.shape
    slots = nz * cap
    hx = nx // NC
    ntp = ny * NC
    anywhere = pl.BlockSpec(memory_space=pl.ANY)
    vmem = pl.BlockSpec(memory_space=pltpu.VMEM)

    def f32(*shape):
        return pltpu.VMEM(shape, F32)

    def bf16(*shape):
        return pltpu.VMEM(shape, BF16)

    outs = pl.pallas_call(
        functools.partial(kernel, nx, nz, ny),
        out_shape=(
            jax.ShapeDtypeStruct((tokens, cols), BF16),
            jax.ShapeDtypeStruct((nx, nz, cap, heads), BF16),
            jax.ShapeDtypeStruct((rank, heads), F32),
            jax.ShapeDtypeStruct((rank, cols), F32),
            jax.ShapeDtypeStruct((1, cap), F32),
        ),
        in_specs=[anywhere] * 6 + [vmem, vmem, vmem, anywhere],
        out_specs=(anywhere, anywhere, anywhere, anywhere, vmem),
        scratch_shapes=[
            bf16(tokens, cols), pltpu.VMEM((heads, cols), jnp.int32), f32(*absmax.shape[::-1]),
            bf16(rank, cols), bf16(tokens, cols), f32(heads, cols),
            bf16(nx, slots, heads), bf16(nx, heads, cols), bf16(nx, rank, heads), bf16(slots, cols),
            f32(rank, slots), f32(rank, slots), f32(ny, rank // ny, slots), f32(ny, rank // ny, slots),
            f32(rank // ny, slots), f32(ny, rank // ny, slots),
            bf16(nx, nz, cap, heads), bf16(hx, nz, cap, heads), bf16(hx, nz, cap, heads),
            bf16(hx, ny, cap, heads), bf16(hx, cap, heads), bf16(nx, nz, cap, heads),
            f32(nz, rank // nz, cols), f32(nz, rank // nz, cols), f32(rank // nz, cols),
            f32(nx, rank // nz, cols), f32(nz, rank // nz, cols),
            bf16(nz, cap, cols), bf16(nz, cap, cols), f32(cap, cols), bf16(tokens, cols),
            f32(nx, rank, heads), f32(nx, rank, heads), f32(rank, heads), f32(rank, cols),
            f32(8, 128), f32(ntp, 8, 128),
            pltpu.SemaphoreType.DMA((N_SEM,)), pltpu.SemaphoreType.DMA((N_SEM,)),
            pltpu.SemaphoreType.DMA((N_LOC,)),
        ],
        compiler_params=pltpu.CompilerParams(
            collective_id=0, has_side_effects=True, vmem_limit_bytes=56 << 20),
        name="block_step",
    )(residual, attention, codes, absmax.T, down.T, up, gate.reshape(1, cap), selected.reshape(1, cap),
      counts.reshape(1, 1), cotangent)
    new_res, head_grad, d_grad, u_grad, g_grad = pl.pallas_call(
        hand_over,
        out_shape=[jax.ShapeDtypeStruct(out.shape, out.dtype) for out in outs],
        in_specs=[anywhere] * 5,
        out_specs=[anywhere] * 5,
        scratch_shapes=[pltpu.VMEM(out.shape, out.dtype) for out in outs]
        + [pltpu.SemaphoreType.DMA((nx + 4,))] * 2,
        name="hand_over",
    )(*outs)
    return new_res, head_grad.reshape(nx * nz * cap, heads), d_grad.T, u_grad, g_grad.reshape(cap)


def solution(mesh):
    return jax.shard_map(
        body,
        mesh=mesh,
        in_specs=(
            P("seq", "tp"),
            P("seq", None),
            P("seq", "tp"),
            P("seq", "tp"),
            P("seq", None),
            P(None, "tp"),
            P("seq"),
            P("seq"),
            P("seq"),
            P("seq", "tp"),
        ),
        out_specs=(P("seq", "tp"), P(None, "seq"), P("seq", None), P(None, "tp"), P("seq")),
        check_vma=False,
    )
```

```python
import functools

import jax
import jax.numpy as jnp
from jax import lax
from jax.experimental import pallas as pl
from jax.experimental.pallas import tpu as pltpu
from jax.sharding import PartitionSpec as P

LEVELS = (
    -1.0,
    -0.6961928009986877,
    -0.5250730514526367,
    -0.39491748809814453,
    -0.28444138169288635,
    -0.18477343022823334,
    -0.09105003625154495,
    0.0,
    0.07958029955625534,
    0.16093020141124725,
    0.24611230194568634,
    0.33791524171829224,
    0.44070982933044434,
    0.5626170039176941,
    0.7229568362236023,
    1.0,
)
adapter_scale = 0.25
F32, BF16 = jnp.float32, jnp.bfloat16
MESH = pl.DeviceIdType.MESH

NX, NZ, NY, NC = 4, 8, 8, 2

(S_G, S_A, S_F0, S_F1, S_AZ, S_W1A, S_W1B, S_W3A, S_W3B, S_W2, S_DT, S_ASIB, S_RSIB, S_RRS, S_RAG,
 S_HSIB, S_HRS, S_FX, S_FSIB, S_URS, S_UX, S_UAG, S_ORS, S_DX, S_GG, N_SEM) = (
    0, 5, 10, 15, 20, *range(22, 32), 32, 34, 36, 38, *range(40, 47))
DIRECT = (S_A, S_F0, S_F1)
(L_COT, L_CODES, L_ABS, L_DOWN, L_UP, L_RES, L_A, L_OUT, L_D, L_U, L_FOUT, L_AG, N_LOC) = (*range(11), 12, 16)


def dot(a, b, ca, cb):
    return lax.dot_general(a, b, (((ca,), (cb,)), ((), ())), preferred_element_type=F32)


def split(value):
    high = value.astype(BF16)
    return high, (value - high.astype(F32)).astype(BF16)


def to_column(row, n):
    at = lax.broadcasted_iota(jnp.int32, (n, n), 0) == lax.broadcasted_iota(jnp.int32, (n, n), 1)
    return jnp.sum(jnp.where(at, jnp.broadcast_to(row, (n, n)), 0.0), axis=1, keepdims=True)


def to_row(column, n):
    at = lax.broadcasted_iota(jnp.int32, (n, n), 0) == lax.broadcasted_iota(jnp.int32, (n, n), 1)
    return jnp.sum(jnp.where(at, jnp.broadcast_to(column, (n, n)), 0.0), axis=0, keepdims=True)


def kernel(nx, nz, ny,
           res_hbm, attn, codes_hbm, abs_hbm, down_hbm, up_hbm, gate_ref, sel_ref, counts_ref, cot_hbm,
           out_res, out_ag, out_d, out_u, out_gate,
           res, codes, absm, up, cot, scales,
           a_all, w_all, dt_all, g_all,
           rt, rt_sib, rt_send, rt_recv, rag_send, rag,
           h_send, h_sib, hs, hr, fx, og,
           u_send, u_recv, ux_send, ux_recv, uag,
           o_send, o_recv, o_home, new_res,
           d_send, d_recv, d_new, u_new, gg_send, gg_recv,
           ssem, rsem, lsem):
    tokens, cols = res.shape
    heads = w_all.shape[1]
    cap = gate_ref.shape[1]
    rank = up.shape[0]
    slots = nz * cap
    hx = nx // NC
    ntp = ny * NC

    seq = lax.axis_index("seq")
    tp = lax.axis_index("tp")
    x, z = seq // nz, seq % nz
    y, c = tp // NC, tp % NC

    def dev_x(k):
        return (((x + k) % nx) * nz + z, tp)

    def dev_z(k):
        return (x * nz + (z + k) % nz, tp)

    def dev_y(k):
        return (seq, ((y + k) % ny) * NC + c)

    def dev_tp(k):
        return (seq, (tp + k) % ntp)

    sibling = (seq, y * NC + (1 - c))

    def send(group, src, dst, device):
        pltpu.make_async_remote_copy(
            src_ref=src, dst_ref=dst, send_sem=ssem.at[group], recv_sem=rsem.at[group],
            device_id=device, device_id_type=MESH,
        ).start()

    def take(group, like):
        pltpu.make_async_copy(like, like, rsem.at[group]).wait()

    def sent(group, like):
        pltpu.make_async_copy(like, like, ssem.at[group]).wait()

    def local(which, src, dst):
        copy = pltpu.make_async_copy(src, dst, lsem.at[which])
        copy.start()
        return copy

    def gather_start(group, n, dev, parts):
        if n == 8 and group in DIRECT:
            for k in (1, 7, 2, 6, 3, 5, 4):
                for src, dst in zip(parts(0, 0), parts(0, k)):
                    send(group, src, dst, dev(k))
            return
        for k in sorted({1, n - 1} | ({2, n - 2} if n == 8 else set())):
            which = {n - 1: 0, 1: 1, n - 2: 2, 2: 3}[n - k] if n > 2 else 0
            for src, dst in zip(parts(0, 0), parts(0, k)):
                send(group + which, src, dst, dev(k))

    def gather_forward(group, n, dev, parts, halves, like):
        if n == 2 or (n == 8 and group in DIRECT):
            return
        far = n // 2 - 2
        for side, which in ((-1, 2 if far else 0), (1, 3 if far else 1)):
            j = side * (far if far else 1)
            take(group + which, like(1))
            if far:
                for src, dst in zip(parts(j, 0), parts(j, -side)):
                    send(group + 4, src, dst, dev(-side))
            half = 0 if side < 0 else 1
            k = -side * (n // 2 - abs(j))
            for src, dst in zip(halves(j, 0, half), halves(j, k, half)):
                send(group + 4, src, dst, dev(k))

    def gather_finish(group, n, like):
        if n == 8 and group in DIRECT:
            take(group, like(n - 1))
            return
        if n != 4:
            take(group, like(1))
        if n == 8:
            take(group + 1, like(1))
        if n > 2:
            take(group + 4, like(n // 2 - 1))

    def gather_sent(group, n, like):
        if n == 8 and group in DIRECT:
            sent(group, like(n - 1))
            return
        for which in range(4 if n == 8 else n // 2):
            sent(group + which, like(1))
        if n > 2:
            sent(group + 4, like(n // 2 - 1))

    def g_parts(j, k):
        return [g_all.at[pl.ds(((j - k) % nz) * cap, cap)]]

    def g_halves(j, k, half):
        return [g_all.at[pl.ds(((j - k) % nz) * cap, cap), pl.ds(half * (cols // 2), cols // 2)]]

    def g_like(n):
        return g_all.at[pl.ds(0, n * cap)]

    def a_part(j, n):
        row = ((y + j + n * (ny // 2)) % nz) * cap
        return a_all.at[hx * c + n, pl.ds(pl.multiple_of(row, cap), cap)]

    def a_parts(j, k):
        return [a_part(j, n) for n in range(hx)]

    def a_halves(j, k, half):
        return [a_part(j, half)]

    def a_like(n):
        return a_all.at[pl.ds(hx * c, hx), pl.ds(0, n * cap)]

    def own(m):
        return jnp.where(c == 0, m, nx - 1 - m)

    def f_row(m):
        return (x + nx - own(m)) % nx

    def f_parts(m):
        return lambda j, k: [fx.at[m] if (j, k) == (0, 0) else og.at[f_row(m), (z + y + j) % nz]]

    def f_halves(m):
        return lambda j, k, half: [
            og.at[f_row(m), (z + y + j) % nz, :, pl.ds(half * (heads // 2), heads // 2)]]

    def f_like(n):
        return og.at[0, pl.ds(0, n)]

    cot_in = local(L_COT, cot_hbm, cot)
    codes_in = local(L_CODES, codes_hbm, codes)
    abs_in = local(L_ABS, abs_hbm, absm)
    down_in = local(L_DOWN, down_hbm, dt_all.at[0])
    up_in = local(L_UP, up_hbm, up)
    res_in = local(L_RES, res_hbm, res)

    barrier = pltpu.get_barrier_semaphore()
    for k in range(1, nx):
        pl.semaphore_signal(barrier, inc=1, device_id=dev_x(k), device_id_type=MESH)
    for k in range(1, nz):
        pl.semaphore_signal(barrier, inc=1, device_id=dev_z(k), device_id_type=MESH)
    for k in range(1, ntp):
        pl.semaphore_signal(barrier, inc=1, device_id=dev_tp(k), device_id_type=MESH)

    gate = to_column(gate_ref[...], cap)
    picked_token = to_column(sel_ref[...].astype(F32), cap)
    live = lax.broadcasted_iota(jnp.int32, (cap, tokens), 0) < counts_ref[...]
    pick = jnp.where(
        live & (lax.broadcasted_iota(jnp.int32, (cap, tokens), 1).astype(F32) == picked_token), 1.0, 0.0)
    pick_bf = pick.astype(BF16)
    cot_in.wait()
    upstream = dot(pick_bf, cot[...], 1, 0)
    g_all[pl.ds(0, cap), :] = (gate * upstream).astype(BF16)

    codes_in.wait()
    abs_in.wait()
    step = 32

    scale_high = absm[...].astype(BF16)
    rest = absm[...] - scale_high.astype(F32)
    scale_mid, scale_low = split(rest)
    qblocks = absm.shape[0]
    spread_to = jnp.where(
        lax.broadcasted_iota(jnp.int32, (qblocks, cols), 1) // (cols // qblocks)
        == lax.broadcasted_iota(jnp.int32, (qblocks, cols), 0), 1.0, 0.0).astype(BF16)
    scales[...] = (dot(scale_high, spread_to, 0, 0) + dot(scale_mid, spread_to, 0, 0)
                   + dot(scale_low, spread_to, 0, 0))

    def dequantize(n, carry):
        rows = pl.ds(pl.multiple_of(n * step, step), step)
        for q in range(cols // 128):
            code = codes[rows, pl.ds(q * 128, 128)]
            b0, b1, b2, b3 = [(code & (1 << bit)) != 0 for bit in range(4)]
            level = LEVELS
            for bit in (b0, b1, b2, b3):
                level = [jnp.where(bit, level[m + 1], level[m]) for m in range(0, len(level), 2)]
            scale = scales[rows, pl.ds(q * 128, 128)]
            w_all[0, rows, pl.ds(q * 128, 128)] = (level[0] * scale).astype(BF16)
        return carry

    lax.fori_loop(0, heads // step, dequantize, 0)
    down_in.wait()

    pl.semaphore_wait(barrier, (nx - 1) + (nz - 1) + (ntp - 1))

    for n in range(hx):
        off = (y + n * (ny // 2)) % nz
        i = hx * c + n
        dest = (z + nz - off) % nz
        at = pl.multiple_of((((x + i) % nx) * nz + dest) * heads, heads)
        block = attn.at[:, pl.ds(at, heads)]
        place = a_all.at[i, pl.ds(pl.multiple_of(off * cap, cap), cap)]

        @pl.when(off == 0)
        def _():
            local(L_A, block, place)

        @pl.when(off != 0)
        def _():
            send(S_AZ + n, block, place, (x * nz + dest, tp))

    gather_start(S_G, nz, dev_z, g_parts)
    hh = heads // 2
    first, second = pl.ds(0, hh), pl.ds(hh, hh)
    send(S_W3A, w_all.at[0, first], w_all.at[3, first], dev_x(1))
    send(S_W1A, w_all.at[0, second], w_all.at[1, second], dev_x(3))
    for k in range(1, nx):
        send(S_DT, dt_all.at[0], dt_all.at[nx - k], dev_x(k))
    send(S_W3B, w_all.at[0, second], w_all.at[3, second], dev_x(1))
    send(S_W1B, w_all.at[0, first], w_all.at[1, first], dev_x(3))

    for n in range(hx):
        off = (y + n * (ny // 2)) % nz

        @pl.when(off == 0)
        def _():
            place = a_all.at[0, pl.ds(0, cap)]
            pltpu.make_async_copy(place, place, lsem.at[L_A]).wait()

        @pl.when(off != 0)
        def _():
            take(S_AZ + n, a_all.at[0, pl.ds(0, cap)])
    gather_start(S_A, ny, dev_y, a_parts)
    gather_forward(S_G, nz, dev_z, g_parts, g_halves, g_like)
    half_w = w_all.at[0, first]
    take(S_W3A, half_w)
    send(S_W2, w_all.at[3, first], w_all.at[2, first], dev_x(1))
    take(S_W1A, half_w)
    send(S_W2, w_all.at[1, second], w_all.at[2, second], dev_x(3))
    gather_forward(S_A, ny, dev_y, a_parts, a_halves, a_like)

    up_in.wait()
    gather_finish(S_G, nz, g_like)
    rt[...] = adapter_scale * dot(up[...], g_all[...], 1, 1)
    send(S_RSIB, rt, rt_sib, sibling)
    rank_part = (adapter_scale * dot(g_all[...], up[...], 1, 1)).astype(BF16)

    def head_block(i):
        part = dot(g_all[...], w_all[i], 1, 1) + dot(rank_part, dt_all[i], 1, 0)
        for j in range(nz):
            h_send[i, j] = part[j * cap:(j + 1) * cap].astype(BF16)

    def head_pair(m):
        send(S_HSIB + m, h_send.at[nx - 1 - own(m)], h_sib.at[m], sibling)

    def head_sum(m):
        take(S_HSIB + m, h_sib.at[m])
        for j in range(nz):
            hs[m, j] = (h_send[own(m), j].astype(F32) + h_sib[m, j].astype(F32)).astype(BF16)
        near = ((x + own(m)) % nx) * nz + z
        for k in (4, 3, 5, 2, 6, 1, 7) if ny == 8 else range(1, ny):
            send(S_HRS + m, hs.at[m, (y + k) % ny], hr.at[m, ny - k], (near, ((y + k) % ny) * NC + c))
        if m == 0:
            @pl.when(c == 0)
            def _():
                hr[0, 0] = hs[0, y]

            @pl.when(c != 0)
            def _():
                send(S_HRS, hs.at[0, y], hr.at[0, 0], (near, tp))
        else:
            send(S_HRS + m, hs.at[m, y], hr.at[m, 0], (near, tp))

    def head_home(m):
        if m == 0:
            @pl.when(c == 0)
            def _():
                take(S_HRS, hr.at[0, pl.ds(1, ny - 1)])

            @pl.when(c != 0)
            def _():
                take(S_HRS, hr.at[0])
        else:
            take(S_HRS + m, hr.at[m])
        total = hr[m, 0].astype(F32)
        for k in range(1, ny):
            total = total + hr[m, k].astype(F32)
        fx[m] = total.astype(BF16)
        local(L_FOUT + m, fx.at[m], og.at[f_row(m), shard_z])
        gather_start(S_F0 + 5 * m, ny, dev_y, f_parts(m))

    def head_forward(m):
        gather_forward(S_F0 + 5 * m, ny, dev_y, f_parts(m), f_halves(m), f_like)

    def head_finish(m):
        gather_finish(S_F0 + 5 * m, ny, f_like)
        pltpu.make_async_copy(fx.at[m], fx.at[m], lsem.at[L_FOUT + m]).wait()
        send(S_FSIB + m, og.at[f_row(m)], og.at[f_row(m)], sibling)
        local(L_AG + m, og.at[f_row(m)], out_ag.at[f_row(m)])

    shard_z = (z + y) % nz
    take(S_DT, dt_all.at[pl.ds(1, nx - 1)])
    head_block(0)
    take(S_W3B, half_w)
    head_block(3)
    head_pair(0)
    take(S_RSIB, rt_sib)
    for j in range(ny):
        rows = pl.ds(j * (rank // ny), rank // ny)
        rt_send[j] = rt[rows, :] + rt_sib[rows, :]
    for k in range(1, ny):
        send(S_RRS, rt_send.at[(y + k) % ny], rt_recv.at[ny - k], dev_y(k))
    take(S_W1B, half_w)
    head_block(1)
    head_sum(0)
    take(S_W2, w_all.at[0])
    head_block(2)
    head_pair(1)
    gather_finish(S_A, ny, a_like)
    a_mine = a_all.at[pl.ds(hx * c, hx)]
    send(S_ASIB, a_mine, a_mine, sibling)
    head_sum(1)
    take(S_RRS, rt_recv.at[pl.ds(1, ny - 1)])
    total = rt_send[y]
    for k in range(1, ny):
        total = total + rt_recv[k]
    rag_send[...] = total.astype(BF16).astype(F32)
    rag[y] = rag_send[...]
    for k in range(1, ny):
        send(S_RAG, rag_send, rag.at[y], dev_y(k))


    take(S_ASIB, a_mine)
    low = jnp.zeros((slots, rank), F32)
    low_t = jnp.zeros((rank, slots), F32)
    for i in range(nx):
        low = low + dot(a_all[i], dt_all[i], 1, 1)
        low_t = low_t + dot(dt_all[i], a_all[i], 1, 1)
    t_high, t_low = split(low_t)
    part = adapter_scale * (dot(t_high, g_all[...], 1, 0) + dot(t_low, g_all[...], 1, 0))
    for j in range(nz):
        u_send[j] = part[j * (rank // nz):(j + 1) * (rank // nz)]
    for k in range(1, nz):
        send(S_URS, u_send.at[(z + k) % nz], u_recv.at[nz - k], dev_z(k))

    high, small = split(adapter_scale * low)
    part = dot(high, up[...], 1, 0) + dot(small, up[...], 1, 0)
    for i in range(nx):
        part = part + dot(a_all[i], w_all[i], 1, 0)
    o_home[...] = part[:cap]
    for j in range(1, nz):
        o_send[j] = part[j * cap:(j + 1) * cap].astype(BF16)
    for k in range(1, nz):
        send(S_ORS, o_send.at[k], o_recv.at[nz - k], dev_z(k))

    head_home(0)
    take(S_URS, u_recv.at[pl.ds(1, nz - 1)])
    total = u_send[z]
    for k in range(1, nz):
        total = total + u_recv[k]
    ux_send[...] = total
    for k in range(1, nx):
        send(S_UX, ux_send, ux_recv.at[nx - k], dev_x(k))

    head_home(1)

    take(S_RAG, rag.at[pl.ds(0, ny - 1)])
    full_rt = jnp.reshape(rag[...], (rank, slots)).astype(BF16)
    for i in range(nx):
        d_send[i] = dot(full_rt, a_all[i], 1, 0)
    for k in range(1, nx):
        send(S_DX, d_send.at[k], d_recv.at[nx - k], dev_x(k))
    head_forward(0)

    head_forward(1)
    take(S_ORS, o_recv.at[pl.ds(1, nz - 1)])
    block = o_home[...]
    for k in range(1, nz):
        block = block + o_recv[k].astype(F32)
    res_in.wait()
    gate_part = to_row(jnp.sum(upstream * block, axis=1, keepdims=True), cap)
    gg_send[...] = jnp.zeros_like(gg_send)
    gg_send[:, pl.ds(0, cap)] = jnp.broadcast_to(gate_part, (8, cap))
    for k in range(1, ntp):
        send(S_GG, gg_send, gg_recv.at[ntp - k], dev_tp(k))
    picked = dot(pick_bf, res[...], 1, 0)
    updated = (picked + gate * block).astype(BF16)
    spread = dot(pick_bf, updated, 0, 0)
    taken = dot(pick_bf, jnp.ones((cap, 128), BF16), 0, 0)[:, :1] > 0.5
    new_res[...] = jnp.where(taken, spread, res[...].astype(F32)).astype(BF16)
    out_copy = local(L_OUT, new_res, out_res)

    head_finish(0)
    take(S_UX, ux_recv.at[pl.ds(1, nx - 1)])
    total = ux_send[...]
    for k in range(1, nx):
        total = total + ux_recv[k]
    ux_send_sum = total
    sent(S_UX, ux_recv.at[pl.ds(1, nx - 1)])
    ux_send[...] = ux_send_sum
    uag[z] = ux_send_sum
    for k in range(1, nz):
        send(S_UAG, ux_send, uag.at[z], dev_z(k))

    take(S_DX, d_recv.at[pl.ds(1, nx - 1)])
    total = d_send[0]
    for k in range(1, nx):
        total = total + d_recv[k]
    d_new[...] = total
    d_copy = local(L_D, d_new, out_d)

    head_finish(1)

    take(S_GG, gg_recv.at[pl.ds(1, ntp - 1)])
    total = gg_send[...]
    for k in range(1, ntp):
        total = total + gg_recv[k]
    out_gate[...] = total[:1, :cap]

    take(S_UAG, uag.at[pl.ds(0, nz - 1)])
    u_new[...] = jnp.reshape(uag[...], (rank, cols))
    u_copy = local(L_U, u_new, out_u)
    for m in range(hx):
        take(S_FSIB + m, og.at[0])
        row = (x + nx - (nx - 1 - own(m))) % nx
        local(L_AG + hx + m, og.at[row], out_ag.at[row])

    for m in range(2 * hx):
        pltpu.make_async_copy(og.at[0], og.at[0], lsem.at[L_AG + m]).wait()
    out_copy.wait()
    d_copy.wait()
    u_copy.wait()
    for n in range(hx):
        @pl.when((y + n * (ny // 2)) % nz != 0)
        def _():
            sent(S_AZ + n, a_all.at[0, pl.ds(0, cap)])
    gather_sent(S_G, nz, g_like)
    gather_sent(S_A, ny, a_like)
    for m in range(hx):
        gather_sent(S_F0 + 5 * m, ny, f_like)
    for group in (S_W1A, S_W1B, S_W3A, S_W3B):
        sent(group, half_w)
    sent(S_W2, w_all.at[0])
    sent(S_DT, dt_all.at[pl.ds(1, nx - 1)])
    sent(S_ASIB, a_mine)
    sent(S_RSIB, rt)
    sent(S_RRS, rt_recv.at[pl.ds(1, ny - 1)])
    sent(S_RAG, rag.at[pl.ds(0, ny - 1)])
    for m in range(hx):
        sent(S_HSIB + m, h_sib.at[m])
        sent(S_FSIB + m, og.at[0])

    @pl.when(c == 0)
    def _():
        sent(S_HRS, hr.at[0, pl.ds(1, ny - 1)])

    @pl.when(c != 0)
    def _():
        sent(S_HRS, hr.at[0])
    sent(S_HRS + 1, hr.at[1])
    sent(S_URS, u_recv.at[pl.ds(1, nz - 1)])
    sent(S_UAG, uag.at[pl.ds(0, nz - 1)])
    sent(S_ORS, o_recv.at[pl.ds(1, nz - 1)])
    sent(S_DX, d_recv.at[pl.ds(1, nx - 1)])
    sent(S_GG, gg_recv.at[pl.ds(1, ntp - 1)])


def hand_over(*refs):
    n = len(refs) // 3
    srcs, dsts, held, into, out_of = refs[:n], refs[n:2 * n], refs[2 * n:3 * n], refs[-2], refs[-1]
    ins, outs = [], []
    for src, dst, mid in zip(srcs, dsts, held):
        pieces = src.shape[0] if len(src.shape) == 4 else 1
        for piece in range(pieces):
            at = pl.ds(piece, 1) if pieces > 1 else slice(None)
            ins.append(pltpu.make_async_copy(src.at[at], mid.at[at], into.at[len(ins)]))
            outs.append(pltpu.make_async_copy(mid.at[at], dst.at[at], out_of.at[len(outs)]))
    for copy in ins:
        copy.start()
    for copy, onward in zip(ins, outs):
        copy.wait()
        onward.start()
    for copy in outs:
        copy.wait()


def body(residual, attention, codes, absmax, down, up, gate, selected, counts, cotangent,
         nx=NX, nz=NZ, ny=NY):
    tokens, cols = residual.shape
    cap = attention.shape[0]
    heads, rank = down.shape
    slots = nz * cap
    hx = nx // NC
    ntp = ny * NC
    anywhere = pl.BlockSpec(memory_space=pl.ANY)
    vmem = pl.BlockSpec(memory_space=pltpu.VMEM)

    def f32(*shape):
        return pltpu.VMEM(shape, F32)

    def bf16(*shape):
        return pltpu.VMEM(shape, BF16)

    outs = pl.pallas_call(
        functools.partial(kernel, nx, nz, ny),
        out_shape=(
            jax.ShapeDtypeStruct((tokens, cols), BF16),
            jax.ShapeDtypeStruct((nx, nz, cap, heads), BF16),
            jax.ShapeDtypeStruct((rank, heads), F32),
            jax.ShapeDtypeStruct((rank, cols), F32),
            jax.ShapeDtypeStruct((1, cap), F32),
        ),
        in_specs=[anywhere] * 6 + [vmem, vmem, vmem, anywhere],
        out_specs=(anywhere, anywhere, anywhere, anywhere, vmem),
        scratch_shapes=[
            bf16(tokens, cols), pltpu.VMEM((heads, cols), jnp.int32), f32(*absmax.shape[::-1]),
            bf16(rank, cols), bf16(tokens, cols), f32(heads, cols),
            bf16(nx, slots, heads), bf16(nx, heads, cols), bf16(nx, rank, heads), bf16(slots, cols),
            f32(rank, slots), f32(rank, slots), f32(ny, rank // ny, slots), f32(ny, rank // ny, slots),
            f32(rank // ny, slots), f32(ny, rank // ny, slots),
            bf16(nx, nz, cap, heads), bf16(hx, nz, cap, heads), bf16(hx, nz, cap, heads),
            bf16(hx, ny, cap, heads), bf16(hx, cap, heads), bf16(nx, nz, cap, heads),
            f32(nz, rank // nz, cols), f32(nz, rank // nz, cols), f32(rank // nz, cols),
            f32(nx, rank // nz, cols), f32(nz, rank // nz, cols),
            bf16(nz, cap, cols), bf16(nz, cap, cols), f32(cap, cols), bf16(tokens, cols),
            f32(nx, rank, heads), f32(nx, rank, heads), f32(rank, heads), f32(rank, cols),
            f32(8, 128), f32(ntp, 8, 128),
            pltpu.SemaphoreType.DMA((N_SEM,)), pltpu.SemaphoreType.DMA((N_SEM,)),
            pltpu.SemaphoreType.DMA((N_LOC,)),
        ],
        compiler_params=pltpu.CompilerParams(
            collective_id=0, has_side_effects=True, vmem_limit_bytes=56 << 20),
        name="block_step",
    )(residual, attention, codes, absmax.T, down.T, up, gate.reshape(1, cap), selected.reshape(1, cap),
      counts.reshape(1, 1), cotangent)
    new_res, head_grad, d_grad, u_grad, g_grad = pl.pallas_call(
        hand_over,
        out_shape=[jax.ShapeDtypeStruct(out.shape, out.dtype) for out in outs],
        in_specs=[anywhere] * 5,
        out_specs=[anywhere] * 5,
        scratch_shapes=[pltpu.VMEM(out.shape, out.dtype) for out in outs]
        + [pltpu.SemaphoreType.DMA((nx + 4,))] * 2,
        name="hand_over",
    )(*outs)
    return new_res, head_grad.reshape(nx * nz * cap, heads), d_grad.T, u_grad, g_grad.reshape(cap)


def solution(mesh):
    return jax.shard_map(
        body,
        mesh=mesh,
        in_specs=(
            P("seq", "tp"),
            P("seq", None),
            P("seq", "tp"),
            P("seq", "tp"),
            P("seq", None),
            P(None, "tp"),
            P("seq"),
            P("seq"),
            P("seq"),
            P("seq", "tp"),
        ),
        out_specs=(P("seq", "tp"), P(None, "seq"), P("seq", None), P(None, "tp"), P("seq")),
        check_vma=False,
    )
```
